512 devices in a mesh: expert: 128 (over y, z, core), dp: 4 (over x).
Axes of the slice: x: 4, y: 4, z: 16, core: 2. Of those that a mesh axis runs over, the one named last changes fastest.
Arguments:
- tokens: bfloat16 [12288, 2048], P(('expert', 'dp')), may hold values from -6 to 6
- route_ids: int32 [12288, 8], P(('expert', 'dp')), may hold values from 0 to 127, all different within a row; in each aligned block of 24 rows (0 to 23, 24 to 47, ...) at most 2 rows name the same one
- gates: float32 [12288, 8], P(('expert', 'dp')), may hold values from 0.05 to 0.5
- cotangent: bfloat16 [12288, 2048], P(('expert', 'dp')), may hold values from -1.5 to 1.5
- w_gate_up: bfloat16 [128, 2048, 768], P('expert', 'dp'), may hold values from -0.125 to 0.125
- w_down: bfloat16 [128, 2048, 384], P('expert', 'dp'), may hold values from -0.3125 to 0.3125
Outputs:
- mixed: bfloat16 [12288, 2048], P(('expert', 'dp'))
- grad_tokens: bfloat16 [12288, 2048], P(('expert', 'dp'))
- grad_gates: float32 [12288, 8], P(('expert', 'dp'))
- grad_gate_up: bfloat16 [128, 2048, 768], P('expert', 'dp')
- grad_down: bfloat16 [128, 2048, 384], P('expert', 'dp')
The draws below stay inside these ranges and needn't reach their ends.
Inputs may be any that keep to these rules, and one draw needn't show every extreme that they name: `route_ids`: each row names 8 different experts. Among the 24 rows of one device no expert is named by more than 2 rows, and in every draw some device's rows name some expert exactly 2 times.
All inputs are finite; a program needn't handle non-finite values.
Results may differ from the reference program's by a relative error of at most 0.0064.
Values may be sent and summed in bfloat16 or wider, within the bound.
A program may use at most 64 MiB of HBM per device.

```python
import math
import jax
import jax.numpy as jnp
import numpy as np
from jax import lax

D = 2048
TOP = 8
FFW = 384
TOK_DEV = 24
EXPERTS = 128
CAP = 2
TOKENS = 12288
N_EXPERT = 128
N_DP = 4


def shard_levels(key, dims, cuts, low, top_value):
    def one(dim, blocks):
        heights = jax.random.uniform(jax.random.fold_in(jax.random.fold_in(key, 6), dim), (blocks,), jnp.float32, low / len(cuts), top_value / len(cuts))
        return jnp.repeat(jnp.exp(heights), dims[dim] // blocks).reshape((-1,) + (1,) * (len(dims) - dim - 1))

    gain = one(*cuts[0])
    for cut in cuts[1:]:
        gain = gain * one(*cut)
    return gain


def routed_block(rng, own, number, rows, count, top, reach, lean):
    order = jax.random.permutation(rng, count)
    heavy_load, usual = shares(count, rows * top, reach, lean, True), shares(count, rows * top, reach, lean, False)
    places = jnp.arange(count)

    def named(tallies, turn):
        used = int((tallies > 0).sum())
        fixed = max(1, used // 4)
        passed = fixed + (places - fixed + turn * (used - fixed)) % max(1, count - fixed)
        return jnp.zeros((count,), jnp.int32).at[order[jnp.where(places < fixed, places, passed)]].set(jnp.asarray(tallies, jnp.int32))

    tallies = jnp.where(number % 4 == 0, named(heavy_load, number // 4), named(usual, number - number // 4 - 1))
    mixed = jax.random.permutation(jax.random.fold_in(own, 3), count)
    giver, taker = mixed[0:count // 2 * 2:2], mixed[1:count // 2 * 2:2]
    slack = jnp.minimum(tallies[giver] - 1, reach - tallies[taker]) // 2
    slack = jnp.where((giver == order[0]) | (taker == order[0]) | (tallies[taker] == 0), 0, jnp.maximum(slack, 0))
    passed = jax.random.randint(jax.random.fold_in(own, 4), (count // 2,), 0, 1 << 20) % (slack + 1)
    tallies = tallies.at[giver].add(-passed).at[taker].add(passed)
    items = jnp.searchsorted(jnp.cumsum(tallies), jnp.arange(rows * top), side="right").astype(jnp.int32)
    table = items.reshape(top, rows).T
    table = table[jax.random.permutation(jax.random.fold_in(own, 1), rows)]
    turn = jax.random.randint(jax.random.fold_in(own, 2), (rows, 1), 0, top)
    return jnp.take_along_axis(table, (jnp.arange(top)[None, :] + turn) % top, axis=1)


def shares(count, total, bound, skew, full):
    loads = [(1 << 20) // math.isqrt(rank ** skew) + 1 for rank in range(1, count + 1)]
    largest = bound if full else min(bound, max(-(-total // count), total * loads[0] // sum(loads)))
    least = 1 if total - largest >= count - 1 else 0
    counts, rest = [largest] + [least] * (count - 1), total - largest - least * (count - 1)
    while rest > 0:
        candidates = [i for i in range(1, count) if counts[i] < largest] or [i for i in range(1, count) if counts[i] < bound]
        whole, budget = sum([loads[i] for i in candidates]), rest
        for i in candidates:
            more = min(bound - counts[i], max(1, budget * loads[i] // whole), rest)
            counts[i] = counts[i] + more
            rest = rest - more
    return np.array(counts)


def centred(own_key, extent, deviation, reach, shards=(), kind=jnp.bfloat16):
    loudness = shard_levels(own_key, extent, shards, -0.22, 0.18) if shards else 1.0
    values = jax.random.normal(own_key, extent, jnp.float32) * deviation * loudness
    return jnp.minimum(jnp.maximum(values, -reach), reach).astype(kind)


def setup_inputs(seed: int = 0) -> dict:
    key_of = jax.random.split(jax.random.key(seed), 7)
    tokens = centred(key_of[0], (TOKENS, D), 1.0, 6.0, ((0, 512),))
    route_ids_keys = jax.random.split(jax.random.fold_in(key_of[1], 1), TOKENS // TOK_DEV)
    route_ids_turns = jax.random.permutation(jax.random.fold_in(key_of[1], 3), TOKENS // TOK_DEV)
    route_ids = jax.vmap(lambda own, number: routed_block(jax.random.fold_in(key_of[1], 2), own, number, TOK_DEV, EXPERTS, TOP, CAP, 2))(route_ids_keys, route_ids_turns).reshape((TOKENS, TOP))
    gates = jnp.clip(0.05 + 0.45 * jax.random.uniform(key_of[2], (TOKENS, TOP), jnp.float32) ** shard_levels(key_of[2], (TOKENS, TOP), ((0, 512),), -0.2, 0.2), 0.05, 0.5)
    cotangent = centred(key_of[3], (TOKENS, D), 0.25, 1.5, ((0, 512),))
    w_gate_up = centred(key_of[4], (EXPERTS, D, 2 * FFW), D ** -0.5, 0.125, ((0, 128), (1, 4)))
    w_down = centred(key_of[5], (EXPERTS, D, FFW), FFW ** -0.5, 0.3125, ((0, 128), (1, 4)))
    return dict(tokens=tokens, route_ids=route_ids, gates=gates, cotangent=cotangent, w_gate_up=w_gate_up, w_down=w_down)


def reference(tokens, route_ids, gates, cotangent, w_gate_up, w_down):
    blocks = N_EXPERT * N_DP
    per_block = TOK_DEV * TOP
    slot_count = N_EXPERT * CAP
    expert_ids = route_ids.reshape(blocks, per_block)
    onehot = (expert_ids[:, :, None] == jnp.arange(EXPERTS, dtype=jnp.int32)[None, None, :]).astype(jnp.int32)
    earlier = jnp.sum((jnp.cumsum(onehot, axis=1, dtype=jnp.int32) - onehot) * onehot, axis=2, dtype=jnp.int32)
    block_index = jnp.arange(blocks, dtype=jnp.int32)
    position = (block_index // N_DP)[:, None] * CAP + earlier
    replica_of = jnp.broadcast_to((block_index % N_DP)[:, None], (blocks, per_block)).astype(jnp.int32)
    assign = jnp.arange(blocks * per_block, dtype=jnp.int32).reshape(blocks, per_block)
    slot_table = jnp.full((EXPERTS, N_DP, slot_count), blocks * per_block, jnp.int32)
    slot_table = slot_table.at[expert_ids, replica_of, position].set(assign)

    tok_pad = jnp.concatenate([tokens, jnp.zeros((1, D), jnp.bfloat16)], axis=0)
    cot_pad = jnp.concatenate([cotangent, jnp.zeros((1, D), jnp.bfloat16)], axis=0)
    gate_pad = jnp.concatenate([gates.reshape(-1), jnp.zeros((1,), jnp.float32)], axis=0)

    def expert_step(totals, inputs):
        mixed_acc, back_acc, score_acc = totals
        slots, weight_in, weight_out = inputs
        sum_gate_up = jnp.zeros((D, 2 * FFW), jnp.float32)
        sum_down = jnp.zeros((D, FFW), jnp.float32)
        for replica in range(N_DP):
            slot_index = slots[replica]
            token_row = slot_index // TOP
            x_rows = tok_pad[token_row]
            dy_rows = cot_pad[token_row]
            weight = gate_pad[slot_index]
            row_grad = (weight[:, None] * dy_rows.astype(jnp.float32)).astype(jnp.bfloat16)
            pre_act = jnp.dot(x_rows, weight_in, preferred_element_type=jnp.float32)
            gate_pre = pre_act[:, :FFW]
            up_pre = pre_act[:, FFW:]
            sigmoid_gate = jax.nn.sigmoid(gate_pre)
            activation = gate_pre * sigmoid_gate
            hidden = (activation * up_pre).astype(jnp.bfloat16)
            expert_out = jnp.dot(hidden, weight_out.T, preferred_element_type=jnp.float32).astype(jnp.bfloat16)
            hidden_grad = jnp.dot(row_grad, weight_out, preferred_element_type=jnp.float32)
            gate_grad = (hidden_grad * up_pre * (sigmoid_gate * (1.0 + gate_pre * (1.0 - sigmoid_gate)))).astype(jnp.bfloat16)
            up_grad = (hidden_grad * activation).astype(jnp.bfloat16)
            pair_grad = jnp.concatenate([gate_grad, up_grad], axis=1)
            input_grad = jnp.dot(pair_grad, weight_in.T, preferred_element_type=jnp.float32).astype(jnp.bfloat16)
            part_gate_up = jnp.dot(x_rows.T, pair_grad, preferred_element_type=jnp.float32).astype(jnp.bfloat16)
            part_down = jnp.dot(row_grad.T, hidden, preferred_element_type=jnp.float32).astype(jnp.bfloat16)
            sum_gate_up = sum_gate_up + lax.optimization_barrier(part_gate_up).astype(jnp.float32)
            sum_down = sum_down + lax.optimization_barrier(part_down).astype(jnp.float32)
            out_wide = expert_out.astype(jnp.float32)
            mixed_acc = mixed_acc.at[token_row].add(weight[:, None] * out_wide)
            back_acc = back_acc.at[token_row].add(input_grad.astype(jnp.float32))
            score_acc = score_acc.at[slot_index].add(jnp.sum(dy_rows.astype(jnp.float32) * out_wide, axis=1))
        return (mixed_acc, back_acc, score_acc), (sum_gate_up.astype(jnp.bfloat16), sum_down.astype(jnp.bfloat16))

    start = (jnp.zeros((TOKENS + 1, D), jnp.float32), jnp.zeros((TOKENS + 1, D), jnp.float32), jnp.zeros((TOKENS * TOP + 1,), jnp.float32))
    totals, grads = lax.scan(expert_step, start, (slot_table, w_gate_up, w_down))
    mixed_acc, back_acc, score_acc = totals
    mixed = mixed_acc[:TOKENS].astype(jnp.bfloat16)
    grad_tokens = back_acc[:TOKENS].astype(jnp.bfloat16)
    grad_gates = score_acc[:TOKENS * TOP].reshape(TOKENS, TOP)
    return (mixed, grad_tokens, grad_gates, grads[0], grads[1])
```

```python
import jax
import jax.numpy as jnp
from jax import lax
from jax.experimental import pallas as pl
from jax.experimental.pallas import tpu as pltpu
from jax.sharding import PartitionSpec as P

NX, NY, NZ, NC = 4, 4, 16, 2
GROUP = NY * NC
HALF = NZ // 2
BATCHES = NZ // 4
PAIR = 2
TOKS = 24
TOP = 8
D = 2048
FFW = 384
LANES = 128
TILE = 512
WIDE = 2 * D + LANES
SHARD = D // NX
SLOTS = GROUP * 4 * PAIR
ROWS = BATCHES * SLOTS
N_SEM = 192
F32 = jnp.float32
BF16 = jnp.bfloat16


def positions():
    order = []
    for b in range(BATCHES):
        s = 2 * b + 1
        order += [s, NZ - s, s + 1, NZ - s - 1 if s + 1 < HALF else 0]
    return {d: i for i, d in enumerate(order)}


POS = positions()


def dot(a, b, contract):
    return lax.dot_general(a, b, ((contract[:1], contract[1:]), ((), ())), preferred_element_type=F32)


def columns(i):
    return pl.ds(pl.multiple_of(i * TILE, TILE), TILE)


def three_parts(v):
    high = v.astype(BF16).astype(F32)
    rest = v - high
    middle = rest.astype(BF16).astype(F32)
    return high, middle, rest - middle


def lane_block(v, shape):
    high, middle, low = three_parts(v)
    lane = lax.broadcasted_iota(jnp.int32, shape, len(shape) - 1)
    return jnp.where(
        lane == 0, high, jnp.where(lane == 1, middle, jnp.where(lane == 2, low, 0.0))
    ).astype(BF16)


def kernel(
    tok, cot, meta, wg, wd,
    mixed, gtok, gg, ggu, gd,
    gx, gc, mb, comb, pb, sel, rows, wgf, wdf, pre, ub, hs, pair, ob, cb,
    part, ggp, dm, um, dd, ud, dg, ug, gp_gu, gp_d, x2_gu, x2_d, x1_gu, x1_d,
    send_sem, recv_sem, local_sem,
):
    e = lax.axis_index("expert")
    x = lax.axis_index("dp")
    plane = NZ * NC
    y = e // plane
    z = (e // NC) % NZ
    c = e % NC
    me = y * NC + c
    up = y * plane + ((z + 1) % NZ) * NC + c
    down = y * plane + ((z + NZ - 1) % NZ) * NC + c
    right = (x + 1) % NX
    left = (x + NX - 1) % NX

    def member(m):
        return (m // NC) * plane + z * NC + m % NC

    barrier = pltpu.get_barrier_semaphore()
    peers = [("expert", up), ("expert", down), ("dp", right), ("dp", left)]
    peers += [("expert", member((me + o) % GROUP)) for o in range(1, GROUP)]
    for axis, target in peers:
        pl.semaphore_signal(
            barrier, inc=1, device_id={axis: target}, device_id_type=pl.DeviceIdType.MESH
        )
    pl.semaphore_wait(barrier, len(peers))

    started = []

    def send(src, dst, axis, target):
        i = len(started)
        copy = pltpu.make_async_remote_copy(
            src_ref=src,
            dst_ref=dst,
            send_sem=send_sem.at[i],
            recv_sem=recv_sem.at[i],
            device_id={axis: target},
            device_id_type=pl.DeviceIdType.MESH,
        )
        copy.start()
        started.append(copy)
        return copy

    halves = [pl.ds(h * (SHARD // 2), SHARD // 2) for h in range(2)]
    ring = {}

    def ring_send(s):
        for name, own, buf in (("x", tok, gx), ("c", cot, gc), ("m", meta, mb)):
            if s <= HALF and not (name == "c" and s == HALF):
                src = own
                if s > 1:
                    ring[name, 1, s - 1].wait_recv()
                    src = buf.at[POS[s - 1]]
                ring[name, 1, s] = send(src, buf.at[POS[s]], "expert", up)
            if s < HALF or (name == "c" and s == HALF):
                src = own
                if s > 1:
                    ring[name, -1, s - 1].wait_recv()
                    src = buf.at[POS[NZ - s + 1]]
                ring[name, -1, s] = send(src, buf.at[POS[NZ - s]], "expert", down)

    ring_send(1)

    weights = ((wg, wgf), (wd, wdf))
    to_right, to_left = {}, {}
    for h in range(2):
        for i, (w, full) in enumerate(weights):
            to_right[i, h] = send(w.at[0, halves[h]], full.at[x, halves[h]], "dp", right)
            g = 1 - h
            to_left[i, g] = send(w.at[0, halves[g]], full.at[x, halves[g]], "dp", left)
    keep = [
        pltpu.make_async_copy(w.at[0], full.at[x], local_sem.at[i])
        for i, (w, full) in enumerate(weights)
    ]
    for copy in keep:
        copy.start()
    on_right, on_left = {}, {}

    def pass_weights():
        for i, (w, full) in enumerate(weights):
            to_right[i, 0].wait_recv()
            piece = full.at[left, halves[0]]
            on_right[i] = send(piece, piece, "dp", right)
            to_left[i, 1].wait_recv()
            piece = full.at[right, halves[1]]
            on_left[i] = send(piece, piece, "dp", left)

    gx[POS[0]] = tok[...]
    gc[POS[0]] = cot[...]
    mb[POS[0]] = meta[...]

    lane = lax.broadcasted_iota(jnp.int32, (LANES, LANES), 1)
    line = lax.broadcasted_iota(jnp.int32, (LANES, LANES), 0)

    def source_of(index):
        total = jnp.zeros(index.shape, jnp.int32)
        for j in range(1, 5):
            total = total + jnp.where(index >= j * TOKS, 1, 0)
        return total

    earlier = jnp.where((line < lane) & (source_of(line) == source_of(lane)), 1.0, 0.0).astype(F32)
    member_line = lax.broadcasted_iota(jnp.int32, (GROUP, LANES), 0)
    expert_line = ((member_line >> 1) * plane + z * NC + (member_line & 1) + 1).astype(F32)
    cube = (GROUP, 4 * PAIR, LANES)
    cube_row = lax.broadcasted_iota(jnp.int32, cube, 1)
    cube_source = source_of(lax.broadcasted_iota(jnp.int32, cube, 2))

    def choose(b):
        tiles = mb[4 * b]
        for j in range(1, 4):
            tiles = tiles + pltpu.roll(mb[4 * b + j], TOKS * j, 1)
        comb[b] = tiles
        hits = jnp.zeros((GROUP, LANES), F32)
        gate = jnp.zeros((GROUP, LANES), F32)
        for k in range(TOP):
            hit = tiles[k : k + 1, :] == expert_line
            hits = hits + jnp.where(hit, 1.0, 0.0)
            gate = gate + jnp.where(hit, tiles[TOP + k : TOP + k + 1, :], 0.0)
        count = dot(hits, earlier, (1, 0))
        wanted = (cube_row >> 1) == cube_source
        turn = (cube_row & 1).astype(F32)
        chosen = jnp.where(
            wanted & (jnp.broadcast_to(count[:, None, :], cube) == turn),
            jnp.broadcast_to(hits[:, None, :], cube),
            0.0,
        )
        pb[b] = chosen.reshape(SLOTS, LANES).astype(BF16)
        weight = jnp.sum(chosen * gate[:, None, :], axis=2, keepdims=True)
        sel[b * GROUP : (b + 1) * GROUP, :, 2 * D :] = lane_block(weight, cube)

    def pick(b, buf, offset):
        take = pb[b][:, : 4 * TOKS]

        @pl.loop(0, D // TILE)
        def _(i):
            block = buf[4 * b : 4 * b + 4, :, columns(i)].reshape(4 * TOKS, TILE)
            got = dot(take, block, (1, 0)).astype(BF16)
            where = pl.ds(pl.multiple_of(offset + i * TILE, TILE), TILE)
            sel[b * GROUP : (b + 1) * GROUP, :, where] = got.reshape(GROUP, 4 * PAIR, TILE)

    def exchange(b, src, dst, sem):
        copies = []
        for o in range(1, GROUP):
            m = (me + o) % GROUP
            copies.append(
                send(src.at[b * GROUP + m], dst.at[b * GROUP + me], "expert", member(m))
            )
        own = pltpu.make_async_copy(src.at[b * GROUP + me], dst.at[b * GROUP + me], sem)
        own.start()
        return copies, own

    def arrive(exchanged):
        for copy in exchanged[0]:
            copy.wait_recv()
        exchanged[1].wait()

    out_rows = {}
    for s in range(2, HALF + 1):
        ring_send(s)
        if s >= 3:
            b = (s - 3) // 2
            if s % 2:
                choose(b)
                pick(b, gx, 0)
            else:
                pick(b, gc, D)
                out_rows[b] = exchange(b, sel, rows, local_sem.at[2 + b])
        if s == 5:
            pass_weights()
    last = BATCHES - 1
    for name, way in (("m", 1), ("x", 1), ("c", -1)):
        ring[name, way, HALF].wait_recv()
    for name, way in (("m", -1), ("x", -1), ("c", 1)):
        ring[name, way, HALF - 1].wait_recv()
    choose(last)
    pick(last, gx, 0)
    pick(last, gc, D)
    out_rows[last] = exchange(last, sel, rows, local_sem.at[2 + last])
    for b in range(BATCHES):
        arrive(out_rows[b])

    def take_rows(offset):
        return rows[:, :, pl.ds(pl.multiple_of(offset, TILE), TILE)].reshape(ROWS, TILE)

    def first_products(slot, first):
        gate_up = dot(take_rows(slot * SHARD), wgf[slot], (1, 0))
        back = dot(take_rows(D + slot * SHARD), wdf[slot], (1, 0))
        if first:
            pre[...] = gate_up
            ub[...] = back
        else:
            pre[...] += gate_up
            ub[...] += back

    for copy in keep:
        copy.wait()
    first_products(x, True)
    for h in range(2):
        for i in range(2):
            to_right[i, h].wait_recv() if h else None
            to_left[i, 1 - h].wait_recv() if h else None
    first_products(left, False)
    first_products(right, False)
    for i in range(2):
        on_right[i].wait_recv()
        on_left[i].wait_recv()
    first_products((x + 2) % NX, False)

    step_rows = 32

    @pl.loop(0, ROWS // step_rows)
    def _(i):
        at = pl.ds(pl.multiple_of(i * step_rows, step_rows), step_rows)
        blocks = pl.ds(i * (step_rows // 8), step_rows // 8)
        gate_pre = pre[at, :FFW]
        up_pre = pre[at, FFW:]
        back = ub[at, :]
        weight = jnp.sum(
            rows[blocks, :, 2 * D :].astype(F32).reshape(step_rows, LANES), axis=1, keepdims=True
        )
        sigmoid_gate = jax.nn.sigmoid(gate_pre)
        activation = gate_pre * sigmoid_gate
        hidden = activation * up_pre
        hidden_grad = weight * back
        hs[at, :] = (weight * hidden).astype(BF16)
        pair[at, :FFW] = (
            hidden_grad * up_pre * (sigmoid_gate * (1.0 + gate_pre * (1.0 - sigmoid_gate)))
        ).astype(BF16)
        pair[at, FFW:] = (hidden_grad * activation).astype(BF16)
        score = jnp.sum(hidden * back, axis=1, keepdims=True)
        ob[blocks, :, 2 * D :] = lane_block(score, (step_rows, LANES)).reshape(
            step_rows // 8, 8, LANES
        )

    def weight_grads(o):
        slot = (x + o) % NX
        gp_gu[o] = dot(take_rows(slot * SHARD), pair[...], (0, 0)).astype(BF16)
        gp_d[o] = dot(take_rows(D + slot * SHARD), hs[...], (0, 0)).astype(BF16)

    grads = ((gp_gu, x2_gu, x1_gu), (gp_d, x2_d, x1_d))
    weight_grads(2)
    far_right, far_left, near = [], [], []
    for gp, x2, x1 in grads:
        far_right.append(send(gp.at[2, halves[0]], x2.at[0], "dp", right))
        far_left.append(send(gp.at[2, halves[1]], x2.at[1], "dp", left))

    @pl.loop(0, NX)
    def _(i):
        out = dot(hs[...], wdf[i], (1, 1)).astype(BF16)
        ob[:, :, columns(i)] = out.reshape(ROWS // 8, 8, TILE)
        back = dot(pair[...], wgf[i], (1, 1)).astype(BF16)
        where = pl.ds(pl.multiple_of(D + i * TILE, TILE), TILE)
        ob[:, :, where] = back.reshape(ROWS // 8, 8, TILE)

    back_rows = {}
    for b in reversed(range(BATCHES)):
        back_rows[b] = exchange(b, ob, cb, local_sem.at[2 + BATCHES + b])
    weight_grads(1)
    weight_grads(3)
    for gp, x2, x1 in grads:
        near.append(send(gp.at[1, halves[1]], x1.at[0, halves[1]], "dp", right))
        near.append(send(gp.at[3, halves[0]], x1.at[1, halves[0]], "dp", left))
    weight_grads(0)

    def pass_grads():
        for i, (gp, x2, x1) in enumerate(grads):
            far_right[i].wait_recv()
            gp[1, halves[0], :] = (gp[1, halves[0], :].astype(F32) + x2[0].astype(F32)).astype(BF16)
            near.append(send(gp.at[1, halves[0]], x1.at[0, halves[0]], "dp", right))
            far_left[i].wait_recv()
            gp[3, halves[1], :] = (gp[3, halves[1], :].astype(F32) + x2[1].astype(F32)).astype(BF16)
            near.append(send(gp.at[3, halves[1]], x1.at[1, halves[1]], "dp", left))

    def combine(b):
        arrive(back_rows[b])
        take = pb[b]

        @pl.loop(0, 2 * D // TILE)
        def _(i):
            got = cb[b * GROUP : (b + 1) * GROUP, :, columns(i)].reshape(SLOTS, TILE)
            total = dot(take, got, (0, 0))
            part[4 * b : 4 * b + 4, :, columns(i)] = total[: 4 * TOKS].reshape(4, TOKS, TILE)

        score = jnp.sum(
            cb[b * GROUP : (b + 1) * GROUP, :, 2 * D :].astype(F32), axis=2, keepdims=True
        )
        spread = jnp.sum(take.astype(F32).reshape(cube) * score, axis=1)
        tiles = comb[b]
        total = jnp.zeros((TOP, LANES), F32)
        for m in range(GROUP):
            hit = tiles[:TOP] == expert_line[m : m + 1, :]
            total = total + jnp.where(hit, spread[m : m + 1, :], 0.0)
        ggp[4 * b] = total
        for j in range(1, 4):
            ggp[4 * b + j] = pltpu.roll(total, LANES - TOKS * j, 1)

    going = {}

    def flow(name, way, q, buf, take, top):
        if q < top:
            going[name, way, q + 1].wait_recv()
            value = buf[q].astype(F32) + take(POS[q if way < 0 else (NZ - q) % NZ])
        else:
            value = take(POS[q if way < 0 else (NZ - q) % NZ])
        buf[q] = value.astype(buf.dtype)
        going[name, way, q] = send(
            buf.at[q], buf.at[q - 1], "expert", down if way < 0 else up
        )

    def mixed_part(p):
        return part[p, :, :D]

    def token_part(p):
        return part[p, :, D:]

    def gate_part(p):
        return ggp[p]

    combine(last)
    for k in range(1, HALF + 1):
        q = HALF + 1 - k
        flow("m", -1, q, dm, mixed_part, HALF)
        flow("t", 1, q, ud, token_part, HALF)
        flow("g", -1, q, dg, gate_part, HALF)
        if k > 1:
            flow("m", 1, q, um, mixed_part, HALF - 1)
            flow("t", -1, q, dd, token_part, HALF - 1)
            flow("g", 1, q, ug, gate_part, HALF - 1)
        if k % 2 == 0 and k < HALF:
            combine(last - k // 2)
        if k == 3:
            pass_grads()

    for way in (-1, 1):
        for name in ("m", "t", "g"):
            going[name, way, 1].wait_recv()
    home = POS[0]
    mixed[...] = (part[home, :, :D] + dm[0].astype(F32) + um[0].astype(F32)).astype(BF16)
    gtok[...] = (part[home, :, D:] + dd[0].astype(F32) + ud[0].astype(F32)).astype(BF16)
    gg[...] = ggp[home] + dg[0] + ug[0]
    for copy in near:
        copy.wait_recv()
    for (gp, x2, x1), out in zip(grads, (ggu, gd)):
        out[0] = (gp[0].astype(F32) + x1[0].astype(F32) + x1[1].astype(F32)).astype(BF16)
    for copy in started:
        copy.wait_send()


def body(tokens, route_ids, gates, cotangent, w_gate_up, w_down):
    pad = ((0, 0), (0, LANES - TOKS))
    meta = jnp.concatenate(
        [jnp.pad(route_ids.T.astype(F32) + 1.0, pad), jnp.pad(gates.T, pad)], axis=0
    )
    vmem = pl.BlockSpec(memory_space=pltpu.VMEM)
    out = pl.pallas_call(
        kernel,
        out_shape=(
            jax.ShapeDtypeStruct((TOKS, D), BF16),
            jax.ShapeDtypeStruct((TOKS, D), BF16),
            jax.ShapeDtypeStruct((TOP, LANES), F32),
            jax.ShapeDtypeStruct((1, SHARD, 2 * FFW), BF16),
            jax.ShapeDtypeStruct((1, SHARD, FFW), BF16),
        ),
        in_specs=[vmem] * 5,
        out_specs=[vmem] * 5,
        scratch_shapes=[
            pltpu.VMEM((NZ, TOKS, D), BF16),
            pltpu.VMEM((NZ, TOKS, D), BF16),
            pltpu.VMEM((NZ, 2 * TOP, LANES), F32),
            pltpu.VMEM((BATCHES, 2 * TOP, LANES), F32),
            pltpu.VMEM((BATCHES, SLOTS, LANES), BF16),
            pltpu.VMEM((ROWS // 8, 8, WIDE), BF16),
            pltpu.VMEM((ROWS // 8, 8, WIDE), BF16),
            pltpu.VMEM((NX, SHARD, 2 * FFW), BF16),
            pltpu.VMEM((NX, SHARD, FFW), BF16),
            pltpu.VMEM((ROWS, 2 * FFW), F32),
            pltpu.VMEM((ROWS, FFW), F32),
            pltpu.VMEM((ROWS, FFW), BF16),
            pltpu.VMEM((ROWS, 2 * FFW), BF16),
            pltpu.VMEM((ROWS // 8, 8, WIDE), BF16),
            pltpu.VMEM((ROWS // 8, 8, WIDE), BF16),
            pltpu.VMEM((NZ, TOKS, 2 * D), F32),
            pltpu.VMEM((NZ, TOP, LANES), F32),
            pltpu.VMEM((HALF + 1, TOKS, D), BF16),
            pltpu.VMEM((HALF, TOKS, D), BF16),
            pltpu.VMEM((HALF, TOKS, D), BF16),
            pltpu.VMEM((HALF + 1, TOKS, D), BF16),
            pltpu.VMEM((HALF + 1, TOP, LANES), F32),
            pltpu.VMEM((HALF, TOP, LANES), F32),
            pltpu.VMEM((NX, SHARD, 2 * FFW), BF16),
            pltpu.VMEM((NX, SHARD, FFW), BF16),
            pltpu.VMEM((2, SHARD // 2, 2 * FFW), BF16),
            pltpu.VMEM((2, SHARD // 2, FFW), BF16),
            pltpu.VMEM((2, SHARD, 2 * FFW), BF16),
            pltpu.VMEM((2, SHARD, FFW), BF16),
            pltpu.SemaphoreType.DMA((N_SEM,)),
            pltpu.SemaphoreType.DMA((N_SEM,)),
            pltpu.SemaphoreType.DMA((2 + 2 * BATCHES,)),
        ],
        compiler_params=pltpu.CompilerParams(
            collective_id=0, has_side_effects=True, vmem_limit_bytes=60 * 1024 * 1024
        ),
        name="routed_layer",
    )(tokens, cotangent, meta, w_gate_up, w_down)
    mixed, grad_tokens, grad_gates, grad_gate_up, grad_down = out
    return mixed, grad_tokens, grad_gates[:, :TOKS].T, grad_gate_up, grad_down


def solution(mesh):
    rows_spec = P(("expert", "dp"), None)
    weight_spec = P("expert", "dp", None)
    return jax.shard_map(
        body,
        mesh=mesh,
        in_specs=(rows_spec, rows_spec, rows_spec, rows_spec, weight_spec, weight_spec),
        out_specs=(rows_spec, rows_spec, rows_spec, weight_spec, weight_spec),
        check_vma=False,
    )
```

```python
import jax
import jax.numpy as jnp
from jax import lax
from jax.experimental import pallas as pl
from jax.experimental.pallas import tpu as pltpu
from jax.sharding import PartitionSpec as P

NX, NY, NZ, NC = 4, 4, 16, 2
GROUP = NY * NC
HALF = NZ // 2
BATCHES = NZ // 4
PAIR = 2
TOKS = 24
TOP = 8
D = 2048
FFW = 384
LANES = 128
TILE = 512
NEXT = D + LANES
WIDE = D + NEXT
SHARD = D // NX
SLOTS = GROUP * 4 * PAIR
ROWS = BATCHES * SLOTS
N_SEM = 296
F32 = jnp.float32
BF16 = jnp.bfloat16


def positions():
    order = []
    for b in range(BATCHES):
        s = 2 * b + 1
        order += [s, NZ - s, s + 1, NZ - s - 1 if s + 1 < HALF else 0]
    return {d: i for i, d in enumerate(order)}


POS = positions()


def dot(a, b, contract):
    return lax.dot_general(a, b, ((contract[:1], contract[1:]), ((), ())), preferred_element_type=F32)


def columns(i, start=0):
    return pl.ds(pl.multiple_of(start + i * TILE, LANES), TILE)


def three_parts(v):
    high = v.astype(BF16).astype(F32)
    rest = v - high
    middle = rest.astype(BF16).astype(F32)
    return high, middle, rest - middle


def lane_block(v, shape):
    high, middle, low = three_parts(v)
    lane = lax.broadcasted_iota(jnp.int32, shape, len(shape) - 1)
    return jnp.where(
        lane == 0, high, jnp.where(lane == 1, middle, jnp.where(lane == 2, low, 0.0))
    ).astype(BF16)


def kernel(
    tok, cot, ids, gates, wg, wd,
    mixed, gtok, gg, ggu, gd,
    gx, gc, mb, comb, pb, sel, rows, wgf, wdf, pre, ub, gb, hs, pair, ob, cb,
    pm, pt, ggp, dm, um, dd, ud, dg, ug, gp_gu, gp_d, x2_gu, x2_d, x1_gu, x1_d,
    send_sem, recv_sem, local_sem,
):
    e = lax.axis_index("expert")
    x = lax.axis_index("dp")
    plane = NZ * NC
    y = e // plane
    z = (e // NC) % NZ
    c = e % NC
    me = y * NC + c
    up = y * plane + ((z + 1) % NZ) * NC + c
    down = y * plane + ((z + NZ - 1) % NZ) * NC + c
    right = (x + 1) % NX
    left = (x + NX - 1) % NX

    def member(m):
        return (m // NC) * plane + z * NC + m % NC

    barrier = pltpu.get_barrier_semaphore()
    peers = [("expert", up), ("expert", down), ("dp", right), ("dp", left)]
    peers += [("expert", member((me + o) % GROUP)) for o in range(1, GROUP)]
    for axis, target in peers:
        pl.semaphore_signal(
            barrier, inc=1, device_id={axis: target}, device_id_type=pl.DeviceIdType.MESH
        )
    pl.semaphore_wait(barrier, len(peers))

    started = []

    def send(src, dst, axis, target):
        i = len(started)
        copy = pltpu.make_async_remote_copy(
            src_ref=src,
            dst_ref=dst,
            send_sem=send_sem.at[i],
            recv_sem=recv_sem.at[i],
            device_id={axis: target},
            device_id_type=pl.DeviceIdType.MESH,
        )
        copy.start()
        started.append(copy)
        return copy

    halves = [pl.ds(h * (SHARD // 2), SHARD // 2) for h in range(2)]
    half_cols = [pl.ds(h * (D // 2), D // 2) for h in range(2)]
    home = POS[0]
    mb[home] = jnp.zeros((2 * TOP, LANES), F32)
    mb[home, :TOP, :TOKS] = ids[...].astype(F32) + 1.0
    mb[home, TOP:, :TOKS] = gates[...]
    chunks = [("m", 0, mb.at[home], mb)]
    chunks += [("x", h, tok, gx) for h in range(2)] + [("c", h, cot, gc) for h in range(2)]
    ring = {}

    def ring_send(s):
        for name, h, own, buf in chunks:
            for way, target in ((1, up), (-1, down)):
                if s > (HALF if (way < 0) == (name == "c") else HALF - 1):
                    continue
                src, dst = own, buf.at[POS[(way * s) % NZ]]
                if s > 1:
                    ring[name, h, way, s - 1].wait_recv()
                    src = buf.at[POS[(way * (s - 1)) % NZ]]
                if name != "m":
                    src, dst = src.at[:, half_cols[h]], dst.at[:, half_cols[h]]
                ring[name, h, way, s] = send(src, dst, "expert", target)

    def ring_wait(name):
        for h in range(1 if name == "m" else 2):
            ring[name, h, 1, HALF - (name == "c")].wait_recv()
            ring[name, h, -1, HALF - (name != "c")].wait_recv()

    ring_send(1)

    weights = ((wg, wgf), (wd, wdf))
    to_right, to_left = {}, {}
    for h in range(2):
        for i, (w, full) in enumerate(weights):
            to_right[i, h] = send(w.at[0, halves[h]], full.at[x, halves[h]], "dp", right)
            g = 1 - h
            to_left[i, g] = send(w.at[0, halves[g]], full.at[x, halves[g]], "dp", left)
    keep = [
        pltpu.make_async_copy(w.at[0], full.at[x], local_sem.at[i])
        for i, (w, full) in enumerate(weights)
    ]
    keep.append(pltpu.make_async_copy(tok, gx.at[home], local_sem.at[2]))
    keep.append(pltpu.make_async_copy(cot, gc.at[home], local_sem.at[3]))
    for copy in keep:
        copy.start()
    on_right, on_left = {}, {}

    def pass_weights():
        for i, (w, full) in enumerate(weights):
            to_right[i, 0].wait_recv()
            piece = full.at[left, halves[0]]
            on_right[i] = send(piece, piece, "dp", right)
            to_left[i, 1].wait_recv()
            piece = full.at[right, halves[1]]
            on_left[i] = send(piece, piece, "dp", left)


    lane = lax.broadcasted_iota(jnp.int32, (LANES, LANES), 1)
    line = lax.broadcasted_iota(jnp.int32, (LANES, LANES), 0)

    def source_of(index):
        total = jnp.zeros(index.shape, jnp.int32)
        for j in range(1, 5):
            total = total + jnp.where(index >= j * TOKS, 1, 0)
        return total

    earlier = jnp.where((line < lane) & (source_of(line) == source_of(lane)), 1.0, 0.0).astype(F32)
    member_line = lax.broadcasted_iota(jnp.int32, (GROUP, LANES), 0)
    expert_line = ((member_line >> 1) * plane + z * NC + (member_line & 1) + 1).astype(F32)
    cube = (GROUP, 4 * PAIR, LANES)
    cube_row = lax.broadcasted_iota(jnp.int32, cube, 1)
    cube_source = source_of(lax.broadcasted_iota(jnp.int32, cube, 2))

    def choose(b):
        tiles = mb[4 * b]
        for j in range(1, 4):
            tiles = tiles + pltpu.roll(mb[4 * b + j], TOKS * j, 1)
        comb[b] = tiles
        hits = jnp.zeros((GROUP, LANES), F32)
        gate = jnp.zeros((GROUP, LANES), F32)
        for k in range(TOP):
            hit = tiles[k : k + 1, :] == expert_line
            hits = hits + jnp.where(hit, 1.0, 0.0)
            gate = gate + jnp.where(hit, tiles[TOP + k : TOP + k + 1, :], 0.0)
        count = dot(hits, earlier, (1, 0))
        wanted = (cube_row >> 1) == cube_source
        turn = (cube_row & 1).astype(F32)
        chosen = jnp.where(
            wanted & (jnp.broadcast_to(count[:, None, :], cube) == turn),
            jnp.broadcast_to(hits[:, None, :], cube),
            0.0,
        )
        pb[b] = chosen.reshape(SLOTS, LANES).astype(BF16)
        weight = jnp.sum(chosen * gate[:, None, :], axis=2, keepdims=True)
        sel[b * GROUP : (b + 1) * GROUP, :, D:NEXT] = lane_block(weight, cube)

    def pick(b, buf, offset):
        take = pb[b][:, : 4 * TOKS]
        batch = slice(b * GROUP, (b + 1) * GROUP)
        weight = jnp.sum(sel[batch, :, D:NEXT].astype(F32), axis=2, keepdims=True)
        for i in range(D // TILE):
            block = buf[4 * b : 4 * b + 4, :, i * TILE : (i + 1) * TILE].reshape(4 * TOKS, TILE)
            got = dot(take, block, (1, 0)).reshape(GROUP, 4 * PAIR, TILE)
            if offset:
                got = got * weight
            sel[batch, :, offset + i * TILE : offset + (i + 1) * TILE] = got.astype(BF16)

    parts = (pl.ds(0, NEXT), pl.ds(NEXT, D))

    def exchange(b, src, dst, part, sem):
        copies = []
        for o in range(1, GROUP):
            m = (me + o) % GROUP
            copies.append(
                send(
                    src.at[b * GROUP + m, :, parts[part]],
                    dst.at[b * GROUP + me, :, parts[part]],
                    "expert",
                    member(m),
                )
            )
        own = pltpu.make_async_copy(
            src.at[b * GROUP + me, :, parts[part]],
            dst.at[b * GROUP + me, :, parts[part]],
            local_sem.at[sem],
        )
        own.start()
        return copies, own

    def arrive(exchanged):
        for copy in exchanged[0]:
            copy.wait_recv()
        exchanged[1].wait()

    out_rows = {}
    for s in range(2, HALF + 1):
        ring_send(s)
        if s >= 3:
            b = (s - 3) // 2
            if s % 2:
                choose(b)
                pick(b, gx, 0)
                out_rows[b, 0] = exchange(b, sel, rows, 0, 4 + 2 * b)
            else:
                pick(b, gc, NEXT)
                out_rows[b, 1] = exchange(b, sel, rows, 1, 5 + 2 * b)
        if s == 5:
            pass_weights()
    last = BATCHES - 1
    for copy in keep:
        copy.wait()
    ring_wait("m")
    choose(last)
    ring_wait("x")
    pick(last, gx, 0)
    out_rows[last, 0] = exchange(last, sel, rows, 0, 4 + 2 * last)
    ring_wait("c")
    pick(last, gc, NEXT)
    out_rows[last, 1] = exchange(last, sel, rows, 1, 5 + 2 * last)
    n_first = len(started)

    def take_rows(i, start=0):
        return rows[:, :, columns(i, start)].reshape(ROWS, TILE)

    def gate_up_product(slot, first):
        value = dot(take_rows(slot), wgf[slot], (1, 0))
        pre[...] = value if first else pre[...] + value

    def down_product(slot, first):
        value = dot(take_rows(slot, NEXT), wdf[slot], (1, 0))
        ub[...] = value if first else ub[...] + value

    for b in range(BATCHES):
        arrive(out_rows[b, 0])
    gate_up_product(x, True)
    for i in range(2):
        to_right[i, 1].wait_recv()
        to_left[i, 0].wait_recv()
    gate_up_product(left, False)
    gate_up_product(right, False)
    for i in range(2):
        on_right[i].wait_recv()
        on_left[i].wait_recv()
    gate_up_product((x + 2) % NX, False)
    for b in range(BATCHES):
        arrive(out_rows[b, 1])
    down_product(0, True)
    for i in range(1, NX):
        down_product(i, False)

    step_rows = 32

    @pl.loop(0, ROWS // step_rows)
    def _(i):
        at = pl.ds(pl.multiple_of(i * step_rows, step_rows), step_rows)
        blocks = pl.ds(i * (step_rows // 8), step_rows // 8)
        gate_pre = pre[at, :FFW]
        up_pre = pre[at, FFW:]
        back = ub[at, :]
        weight = jnp.sum(
            rows[blocks, :, D:NEXT].astype(F32).reshape(step_rows, LANES), axis=1, keepdims=True
        )
        sigmoid_gate = jax.nn.sigmoid(gate_pre)
        activation = gate_pre * sigmoid_gate
        hidden = activation * up_pre
        gb[at, :] = jnp.broadcast_to(weight, (step_rows, LANES))
        hs[at, :] = hidden.astype(BF16)
        pair[at, :FFW] = (
            back * up_pre * (sigmoid_gate * (1.0 + gate_pre * (1.0 - sigmoid_gate)))
        ).astype(BF16)
        pair[at, FFW:] = (back * activation).astype(BF16)
        score = jnp.sum(hidden * back, axis=1, keepdims=True)
        score = score / jnp.where(weight > 0.0, weight, 1.0)
        ob[blocks, :, D:NEXT] = lane_block(score, (step_rows, LANES)).reshape(
            step_rows // 8, 8, LANES
        )

    def send_back(b, part):
        return exchange(b, ob, cb, part, 4 + 2 * BATCHES + 2 * b + part)

    last = BATCHES - 1
    back_rows = {}
    scale = gb[:, :1]
    for i in range(NX):
        out = (dot(hs[...], wdf[i], (1, 1)) * scale).astype(BF16)
        ob[:, :, i * TILE : (i + 1) * TILE] = out.reshape(ROWS // 8, 8, TILE)
    back_rows[last, 0] = send_back(last, 0)
    for i in range(NX):
        back = dot(pair[...], wgf[i], (1, 1)).astype(BF16)
        ob[:, :, NEXT + i * TILE : NEXT + (i + 1) * TILE] = back.reshape(ROWS // 8, 8, TILE)
    back_rows[last, 1] = send_back(last, 1)

    def weight_grads(o):
        slot = (x + o) % NX
        gp_gu[o] = dot(take_rows(slot), pair[...], (0, 0)).astype(BF16)
        gp_d[o] = dot(take_rows(slot, NEXT), hs[...], (0, 0)).astype(BF16)

    grads = ((gp_gu, x2_gu, x1_gu), (gp_d, x2_d, x1_d))
    far_right, far_left, near = [], [], []

    def far_grads():
        weight_grads(2)
        for gp, x2, x1 in grads:
            far_right.append(send(gp.at[2, halves[0]], x2.at[0], "dp", right))
            far_left.append(send(gp.at[2, halves[1]], x2.at[1], "dp", left))

    def right_grads():
        weight_grads(1)
        for gp, x2, x1 in grads:
            near.append(send(gp.at[1, halves[1]], x1.at[0, halves[1]], "dp", right))

    def left_grads():
        weight_grads(3)
        for gp, x2, x1 in grads:
            near.append(send(gp.at[3, halves[0]], x1.at[1, halves[0]], "dp", left))

    def pass_grads():
        for i, (gp, x2, x1) in enumerate(grads):
            far_right[i].wait_recv()
            gp[1, halves[0], :] = (gp[1, halves[0], :].astype(F32) + x2[0].astype(F32)).astype(BF16)
            near.append(send(gp.at[1, halves[0]], x1.at[0, halves[0]], "dp", right))
            far_left[i].wait_recv()
            gp[3, halves[1], :] = (gp[3, halves[1], :].astype(F32) + x2[1].astype(F32)).astype(BF16)
            near.append(send(gp.at[3, halves[1]], x1.at[1, halves[1]], "dp", left))

    def combine(b, part):
        arrive(back_rows[b, part])
        take = pb[b]
        batch = slice(b * GROUP, (b + 1) * GROUP)
        start, total = ((0, pm), (NEXT, pt))[part]
        for i in range(D // TILE):
            got = cb[batch, :, start + i * TILE : start + (i + 1) * TILE].reshape(SLOTS, TILE)
            value = dot(take, got, (0, 0))[: 4 * TOKS].reshape(4, TOKS, TILE)
            total[4 * b : 4 * b + 4, :, i * TILE : (i + 1) * TILE] = value
        if part:
            return
        score = jnp.sum(cb[batch, :, D:NEXT].astype(F32), axis=2, keepdims=True)
        spread = jnp.sum(take.astype(F32).reshape(cube) * score, axis=1)
        tiles = comb[b]
        total = jnp.zeros((TOP, LANES), F32)
        for m in range(GROUP):
            hit = tiles[:TOP] == expert_line[m : m + 1, :]
            total = total + jnp.where(hit, spread[m : m + 1, :], 0.0)
        ggp[4 * b] = total
        for j in range(1, 4):
            ggp[4 * b + j] = pltpu.roll(total, LANES - TOKS * j, 1)

    going = {}

    def flow(name, way, q, buf, total, top, h=None):
        cols = slice(None) if h is None else slice(h * (D // 2), (h + 1) * (D // 2))
        value = total[POS[q if way < 0 else (NZ - q) % NZ], :, cols]
        if q < top:
            going[name, way, h, q + 1].wait_recv()
            value = value + buf[q, :, cols].astype(F32)
        buf[q, :, cols] = value.astype(buf.dtype)
        src, dst = buf.at[q], buf.at[q - 1]
        if h is not None:
            src, dst = src.at[:, half_cols[h]], dst.at[:, half_cols[h]]
        going[name, way, h, q] = send(src, dst, "expert", down if way < 0 else up)

    def step(k):
        q = HALF + 1 - k
        for h in range(2):
            flow("m", -1, q, dm, pm, HALF, h)
            if k > 1:
                flow("m", 1, q, um, pm, HALF - 1, h)
        flow("g", -1, q, dg, ggp, HALF)
        if k > 1:
            flow("g", 1, q, ug, ggp, HALF - 1)
        else:
            combine(last, 1)
        for h in range(2):
            flow("t", 1, q, ud, pt, HALF, h)
            if k > 1:
                flow("t", -1, q, dd, pt, HALF - 1, h)

    settled = []

    def settle(count):
        for copy in started[len(settled) : count]:
            copy.wait_send()
            settled.append(copy)

    far_grads()
    back_rows[last - 1, 0] = send_back(last - 1, 0)
    back_rows[last - 1, 1] = send_back(last - 1, 1)
    combine(last, 0)
    step(1)
    for b in reversed(range(last - 1)):
        back_rows[b, 0] = send_back(b, 0)
        back_rows[b, 1] = send_back(b, 1)
    right_grads()
    step(2)
    left_grads()
    combine(last - 1, 0)
    combine(last - 1, 1)
    step(3)
    weight_grads(0)
    settle(n_first)
    step(4)
    combine(last - 2, 0)
    combine(last - 2, 1)
    step(5)
    pass_grads()
    step(6)
    combine(last - 3, 0)
    combine(last - 3, 1)
    step(7)
    settle(len(started) - 60)
    step(8)

    for key, copy in going.items():
        if key[-1] == 1:
            copy.wait_recv()
    mixed[...] = (pm[home] + dm[0].astype(F32) + um[0].astype(F32)).astype(BF16)
    gtok[...] = (pt[home] + dd[0].astype(F32) + ud[0].astype(F32)).astype(BF16)
    gg[...] = ggp[home] + dg[0] + ug[0]
    for copy in near:
        copy.wait_recv()
    for (gp, x2, x1), out in zip(grads, (ggu, gd)):
        out[0] = (gp[0].astype(F32) + x1[0].astype(F32) + x1[1].astype(F32)).astype(BF16)
    settle(len(started))


def hand_over(m, t, g, u, d, m_out, t_out, g_out, u_out, d_out, mv, tv, uv, dv, sem, sem_out):
    arrays = ((u, uv, u_out), (d, dv, d_out), (m, mv, m_out), (t, tv, t_out))
    loads = [pltpu.make_async_copy(a, v, sem.at[i]) for i, (a, v, o) in enumerate(arrays)]
    for copy in loads:
        copy.start()
    g_out[...] = g[:, :TOKS]
    stores = []
    for i, (a, v, o) in enumerate(arrays):
        loads[i].wait()
        stores.append(pltpu.make_async_copy(v, o, sem_out.at[i]))
        stores[i].start()
    for copy in stores:
        copy.wait()


def body(tokens, route_ids, gates, cotangent, w_gate_up, w_down):
    vmem = pl.BlockSpec(memory_space=pltpu.VMEM)
    hbm = pl.BlockSpec(memory_space=pl.ANY)
    out = pl.pallas_call(
        kernel,
        out_shape=(
            jax.ShapeDtypeStruct((TOKS, D), BF16),
            jax.ShapeDtypeStruct((TOKS, D), BF16),
            jax.ShapeDtypeStruct((TOP, LANES), F32),
            jax.ShapeDtypeStruct((1, SHARD, 2 * FFW), BF16),
            jax.ShapeDtypeStruct((1, SHARD, FFW), BF16),
        ),
        in_specs=[hbm, hbm, vmem, vmem, hbm, hbm],
        out_specs=[vmem] * 5,
        scratch_shapes=[
            pltpu.VMEM((NZ, TOKS, D), BF16),
            pltpu.VMEM((NZ, TOKS, D), BF16),
            pltpu.VMEM((NZ, 2 * TOP, LANES), F32),
            pltpu.VMEM((BATCHES, 2 * TOP, LANES), F32),
            pltpu.VMEM((BATCHES, SLOTS, LANES), BF16),
            pltpu.VMEM((ROWS // 8, 8, WIDE), BF16),
            pltpu.VMEM((ROWS // 8, 8, WIDE), BF16),
            pltpu.VMEM((NX, SHARD, 2 * FFW), BF16),
            pltpu.VMEM((NX, SHARD, FFW), BF16),
            pltpu.VMEM((ROWS, 2 * FFW), F32),
            pltpu.VMEM((ROWS, FFW), F32),
            pltpu.VMEM((ROWS, LANES), F32),
            pltpu.VMEM((ROWS, FFW), BF16),
            pltpu.VMEM((ROWS, 2 * FFW), BF16),
            pltpu.VMEM((ROWS // 8, 8, WIDE), BF16),
            pltpu.VMEM((ROWS // 8, 8, WIDE), BF16),
            pltpu.VMEM((NZ, TOKS, D), F32),
            pltpu.VMEM((NZ, TOKS, D), F32),
            pltpu.VMEM((NZ, TOP, LANES), F32),
            pltpu.VMEM((HALF + 1, TOKS, D), BF16),
            pltpu.VMEM((HALF, TOKS, D), BF16),
            pltpu.VMEM((HALF, TOKS, D), BF16),
            pltpu.VMEM((HALF + 1, TOKS, D), BF16),
            pltpu.VMEM((HALF + 1, TOP, LANES), F32),
            pltpu.VMEM((HALF, TOP, LANES), F32),
            pltpu.VMEM((NX, SHARD, 2 * FFW), BF16),
            pltpu.VMEM((NX, SHARD, FFW), BF16),
            pltpu.VMEM((2, SHARD // 2, 2 * FFW), BF16),
            pltpu.VMEM((2, SHARD // 2, FFW), BF16),
            pltpu.VMEM((2, SHARD, 2 * FFW), BF16),
            pltpu.VMEM((2, SHARD, FFW), BF16),
            pltpu.SemaphoreType.DMA((N_SEM,)),
            pltpu.SemaphoreType.DMA((N_SEM,)),
            pltpu.SemaphoreType.DMA((4 + 4 * BATCHES,)),
        ],
        compiler_params=pltpu.CompilerParams(
            collective_id=0, has_side_effects=True, vmem_limit_bytes=60 * 1024 * 1024
        ),
        name="routed_layer",
    )(tokens, cotangent, route_ids.T, gates.T, w_gate_up, w_down)
    specs = [hbm, hbm, vmem, hbm, hbm]
    mixed, grad_tokens, grad_gates, grad_gate_up, grad_down = pl.pallas_call(
        hand_over,
        out_shape=(
            jax.ShapeDtypeStruct((TOKS, D), BF16),
            jax.ShapeDtypeStruct((TOKS, D), BF16),
            jax.ShapeDtypeStruct((TOP, TOKS), F32),
            jax.ShapeDtypeStruct((1, SHARD, 2 * FFW), BF16),
            jax.ShapeDtypeStruct((1, SHARD, FFW), BF16),
        ),
        in_specs=specs,
        out_specs=specs,
        scratch_shapes=[
            pltpu.VMEM((TOKS, D), BF16),
            pltpu.VMEM((TOKS, D), BF16),
            pltpu.VMEM((1, SHARD, 2 * FFW), BF16),
            pltpu.VMEM((1, SHARD, FFW), BF16),
            pltpu.SemaphoreType.DMA((4,)),
            pltpu.SemaphoreType.DMA((4,)),
        ],
        name="hand_over",
    )(*out)
    return mixed, grad_tokens, grad_gates.T, grad_gate_up, grad_down


def solution(mesh):
    rows_spec = P(("expert", "dp"), None)
    weight_spec = P("expert", "dp", None)
    return jax.shard_map(
        body,
        mesh=mesh,
        in_specs=(rows_spec, rows_spec, rows_spec, rows_spec, weight_spec, weight_spec),
        out_specs=(rows_spec, rows_spec, rows_spec, weight_spec, weight_spec),
        check_vma=False,
    )
```

```python
import jax
import jax.numpy as jnp
from jax import lax
from jax.experimental import pallas as pl
from jax.experimental.pallas import tpu as pltpu
from jax.sharding import PartitionSpec as P

NX, NY, NZ, NC = 4, 4, 16, 2
GROUP = NY * NC
HALF = NZ // 2
BATCHES = NZ // 4
PAIR = 2
TOKS = 24
TOP = 8
D = 2048
FFW = 384
LANES = 128
TILE = 512
NEXT = D + LANES
WIDE = D + NEXT
SHARD = D // NX
SLOTS = GROUP * 4 * PAIR
ROWS = BATCHES * SLOTS
N_SEM = 296
F32 = jnp.float32
BF16 = jnp.bfloat16


def positions():
    order = []
    for b in range(BATCHES):
        s = 2 * b + 1
        order += [s, NZ - s, s + 1, NZ - s - 1 if s + 1 < HALF else 0]
    return {d: i for i, d in enumerate(order)}


POS = positions()


def dot(a, b, contract):
    return lax.dot_general(a, b, ((contract[:1], contract[1:]), ((), ())), preferred_element_type=F32)


def columns(i, start=0):
    return pl.ds(pl.multiple_of(start + i * TILE, LANES), TILE)


def three_parts(v):
    high = v.astype(BF16).astype(F32)
    rest = v - high
    middle = rest.astype(BF16).astype(F32)
    return high, middle, rest - middle


def lane_block(v, shape):
    high, middle, low = three_parts(v)
    lane = lax.broadcasted_iota(jnp.int32, shape, len(shape) - 1)
    return jnp.where(
        lane == 0, high, jnp.where(lane == 1, middle, jnp.where(lane == 2, low, 0.0))
    ).astype(BF16)


def kernel(
    tok, cot, ids, gates, wg, wd,
    mixed, gtok, gg, ggu, gd,
    gx, gc, mb, comb, pb, sel, rows, wgf, wdf, pre, ub, gb, hs, pair, ob, cb,
    pm, pt, ggp, dm, um, dd, ud, dg, ug, gp_gu, gp_d, x2_gu, x2_d, x1_gu, x1_d, fm, ft,
    send_sem, recv_sem, local_sem,
):
    e = lax.axis_index("expert")
    x = lax.axis_index("dp")
    plane = NZ * NC
    y = e // plane
    z = (e // NC) % NZ
    c = e % NC
    me = y * NC + c
    up = y * plane + ((z + 1) % NZ) * NC + c
    down = y * plane + ((z + NZ - 1) % NZ) * NC + c
    right = (x + 1) % NX
    left = (x + NX - 1) % NX

    def member(m):
        return (m // NC) * plane + z * NC + m % NC

    barrier = pltpu.get_barrier_semaphore()
    peers = [("expert", up), ("expert", down), ("dp", right), ("dp", left)]
    peers += [("expert", member((me + o) % GROUP)) for o in range(1, GROUP)]
    for axis, target in peers:
        pl.semaphore_signal(
            barrier, inc=1, device_id={axis: target}, device_id_type=pl.DeviceIdType.MESH
        )
    pl.semaphore_wait(barrier, len(peers))

    started = []

    def send(src, dst, axis, target):
        i = len(started)
        copy = pltpu.make_async_remote_copy(
            src_ref=src,
            dst_ref=dst,
            send_sem=send_sem.at[i],
            recv_sem=recv_sem.at[i],
            device_id={axis: target},
            device_id_type=pl.DeviceIdType.MESH,
        )
        copy.start()
        started.append(copy)
        return copy

    halves = [pl.ds(h * (SHARD // 2), SHARD // 2) for h in range(2)]
    half_cols = [pl.ds(h * (D // 2), D // 2) for h in range(2)]
    home = POS[0]
    mb[home] = jnp.zeros((2 * TOP, LANES), F32)
    mb[home, :TOP, :TOKS] = ids[...].astype(F32) + 1.0
    mb[home, TOP:, :TOKS] = gates[...]
    chunks = [("x", 0, tok, gx), ("x", 1, tok, gx), ("m", 0, mb.at[home], mb)]
    chunks += [("c", 0, cot, gc), ("c", 1, cot, gc)]
    ring = {}

    def reach(way, h):
        return HALF if (way > 0) == (h == 0) else HALF - 1

    def ring_send(s):
        for name, h, own, buf in chunks:
            for way, target in ((1, up), (-1, down)):
                if s > reach(way, h):
                    continue
                src, dst = own, buf.at[POS[(way * s) % NZ]]
                if s > 1:
                    ring[name, h, way, s - 1].wait_recv()
                    src = buf.at[POS[(way * (s - 1)) % NZ]]
                if name != "m":
                    src, dst = src.at[:, half_cols[h]], dst.at[:, half_cols[h]]
                ring[name, h, way, s] = send(src, dst, "expert", target)

    def ring_wait(name):
        for h in range(1 if name == "m" else 2):
            ring[name, h, 1, reach(1, h)].wait_recv()
            ring[name, h, -1, reach(-1, h)].wait_recv()

    ring_send(1)

    weights = ((wg, wgf), (wd, wdf))
    to_right, to_left = {}, {}
    for h in range(2):
        for i, (w, full) in enumerate(weights):
            to_right[i, h] = send(w.at[0, halves[h]], full.at[x, halves[h]], "dp", right)
            g = 1 - h
            to_left[i, g] = send(w.at[0, halves[g]], full.at[x, halves[g]], "dp", left)
    keep = [
        pltpu.make_async_copy(w.at[0], full.at[x], local_sem.at[i])
        for i, (w, full) in enumerate(weights)
    ]
    keep.append(pltpu.make_async_copy(tok, gx.at[home], local_sem.at[2]))
    keep.append(pltpu.make_async_copy(cot, gc.at[home], local_sem.at[3]))
    for copy in keep:
        copy.start()
    on_right, on_left = {}, {}

    def pass_weights():
        for i, (w, full) in enumerate(weights):
            to_right[i, 0].wait_recv()
            piece = full.at[left, halves[0]]
            on_right[i] = send(piece, piece, "dp", right)
            to_left[i, 1].wait_recv()
            piece = full.at[right, halves[1]]
            on_left[i] = send(piece, piece, "dp", left)


    lane = lax.broadcasted_iota(jnp.int32, (LANES, LANES), 1)
    line = lax.broadcasted_iota(jnp.int32, (LANES, LANES), 0)

    def source_of(index):
        total = jnp.zeros(index.shape, jnp.int32)
        for j in range(1, 5):
            total = total + jnp.where(index >= j * TOKS, 1, 0)
        return total

    earlier = jnp.where((line < lane) & (source_of(line) == source_of(lane)), 1.0, 0.0).astype(F32)
    member_line = lax.broadcasted_iota(jnp.int32, (GROUP, LANES), 0)
    expert_line = ((member_line >> 1) * plane + z * NC + (member_line & 1) + 1).astype(F32)
    cube = (GROUP, 4 * PAIR, LANES)
    cube_row = lax.broadcasted_iota(jnp.int32, cube, 1)
    cube_source = source_of(lax.broadcasted_iota(jnp.int32, cube, 2))

    def choose(b):
        tiles = mb[4 * b]
        for j in range(1, 4):
            tiles = tiles + pltpu.roll(mb[4 * b + j], TOKS * j, 1)
        comb[b] = tiles
        hits = jnp.zeros((GROUP, LANES), F32)
        gate = jnp.zeros((GROUP, LANES), F32)
        for k in range(TOP):
            hit = tiles[k : k + 1, :] == expert_line
            hits = hits + jnp.where(hit, 1.0, 0.0)
            gate = gate + jnp.where(hit, tiles[TOP + k : TOP + k + 1, :], 0.0)
        count = dot(hits, earlier, (1, 0))
        wanted = (cube_row >> 1) == cube_source
        turn = (cube_row & 1).astype(F32)
        chosen = jnp.where(
            wanted & (jnp.broadcast_to(count[:, None, :], cube) == turn),
            jnp.broadcast_to(hits[:, None, :], cube),
            0.0,
        )
        pb[b] = chosen.reshape(SLOTS, LANES).astype(BF16)
        weight = jnp.sum(chosen * gate[:, None, :], axis=2, keepdims=True)
        sel[b * GROUP : (b + 1) * GROUP, :, D:NEXT] = lane_block(weight, cube)

    def pick(b, buf, offset):
        take = pb[b][:, : 4 * TOKS]
        batch = slice(b * GROUP, (b + 1) * GROUP)
        weight = jnp.sum(sel[batch, :, D:NEXT].astype(F32), axis=2, keepdims=True)
        for i in range(D // TILE):
            block = buf[4 * b : 4 * b + 4, :, i * TILE : (i + 1) * TILE].reshape(4 * TOKS, TILE)
            got = dot(take, block, (1, 0)).reshape(GROUP, 4 * PAIR, TILE)
            if offset:
                got = got * weight
            sel[batch, :, offset + i * TILE : offset + (i + 1) * TILE] = got.astype(BF16)

    parts = (pl.ds(0, NEXT), pl.ds(NEXT, D))

    def exchange(b, src, dst, part, sem):
        copies = []
        for o in range(1, GROUP):
            m = (me + o) % GROUP
            copies.append(
                send(
                    src.at[b * GROUP + m, :, parts[part]],
                    dst.at[b * GROUP + me, :, parts[part]],
                    "expert",
                    member(m),
                )
            )
        own = pltpu.make_async_copy(
            src.at[b * GROUP + me, :, parts[part]],
            dst.at[b * GROUP + me, :, parts[part]],
            local_sem.at[sem],
        )
        own.start()
        return copies, own

    def arrive(exchanged):
        for copy in exchanged[0]:
            copy.wait_recv()
        exchanged[1].wait()

    out_rows = {}
    for s in range(2, HALF + 1):
        ring_send(s)
        if s >= 3:
            b = (s - 3) // 2
            if s % 2:
                choose(b)
                pick(b, gx, 0)
                out_rows[b, 0] = exchange(b, sel, rows, 0, 4 + 2 * b)
            else:
                pick(b, gc, NEXT)
                out_rows[b, 1] = exchange(b, sel, rows, 1, 5 + 2 * b)
        if s == 5:
            pass_weights()
    last = BATCHES - 1
    for copy in keep:
        copy.wait()
    ring_wait("m")
    choose(last)
    ring_wait("x")
    pick(last, gx, 0)
    out_rows[last, 0] = exchange(last, sel, rows, 0, 4 + 2 * last)
    ring_wait("c")
    pick(last, gc, NEXT)
    out_rows[last, 1] = exchange(last, sel, rows, 1, 5 + 2 * last)
    n_first = len(started)

    def take_rows(i, start=0):
        return rows[:, :, columns(i, start)].reshape(ROWS, TILE)

    def gate_up_product(slot, first):
        value = dot(take_rows(slot), wgf[slot], (1, 0))
        pre[...] = value if first else pre[...] + value

    def down_product(slot, first):
        value = dot(take_rows(slot, NEXT), wdf[slot], (1, 0))
        ub[...] = value if first else ub[...] + value

    for b in range(BATCHES):
        arrive(out_rows[b, 0])
    gate_up_product(x, True)
    for i in range(2):
        to_right[i, 1].wait_recv()
        to_left[i, 0].wait_recv()
    gate_up_product(left, False)
    gate_up_product(right, False)
    for i in range(2):
        on_right[i].wait_recv()
        on_left[i].wait_recv()
    gate_up_product((x + 2) % NX, False)
    for b in range(BATCHES):
        arrive(out_rows[b, 1])
    down_product(0, True)
    for i in range(1, NX):
        down_product(i, False)

    step_rows = 32

    @pl.loop(0, ROWS // step_rows)
    def _(i):
        at = pl.ds(pl.multiple_of(i * step_rows, step_rows), step_rows)
        blocks = pl.ds(i * (step_rows // 8), step_rows // 8)
        gate_pre = pre[at, :FFW]
        up_pre = pre[at, FFW:]
        back = ub[at, :]
        weight = jnp.sum(
            rows[blocks, :, D:NEXT].astype(F32).reshape(step_rows, LANES), axis=1, keepdims=True
        )
        sigmoid_gate = jax.nn.sigmoid(gate_pre)
        activation = gate_pre * sigmoid_gate
        hidden = activation * up_pre
        gb[at, :] = jnp.broadcast_to(weight, (step_rows, LANES))
        hs[at, :] = hidden.astype(BF16)
        pair[at, :FFW] = (
            back * up_pre * (sigmoid_gate * (1.0 + gate_pre * (1.0 - sigmoid_gate)))
        ).astype(BF16)
        pair[at, FFW:] = (back * activation).astype(BF16)
        score = jnp.sum(hidden * back, axis=1, keepdims=True)
        score = score / jnp.where(weight > 0.0, weight, 1.0)
        ob[blocks, :, D:NEXT] = lane_block(score, (step_rows, LANES)).reshape(
            step_rows // 8, 8, LANES
        )

    def send_back(b, part):
        return exchange(b, ob, cb, part, 4 + 2 * BATCHES + 2 * b + part)

    def weight_grads(o):
        slot = (x + o) % NX
        gp_gu[o] = dot(take_rows(slot), pair[...], (0, 0)).astype(BF16)
        gp_d[o] = dot(take_rows(slot, NEXT), hs[...], (0, 0)).astype(BF16)

    grads = ((gp_gu, x2_gu, x1_gu), (gp_d, x2_d, x1_d))
    far_right, far_left, near = [], [], []

    def far_grads():
        weight_grads(2)
        for gp, x2, x1 in grads:
            far_right.append(send(gp.at[2, halves[0]], x2.at[0], "dp", right))
            far_left.append(send(gp.at[2, halves[1]], x2.at[1], "dp", left))

    def right_grads():
        weight_grads(1)
        for gp, x2, x1 in grads:
            near.append(send(gp.at[1, halves[1]], x1.at[0, halves[1]], "dp", right))

    def left_grads():
        weight_grads(3)
        for gp, x2, x1 in grads:
            near.append(send(gp.at[3, halves[0]], x1.at[1, halves[0]], "dp", left))

    def pass_grads():
        for i, (gp, x2, x1) in enumerate(grads):
            far_right[i].wait_recv()
            gp[1, halves[0], :] = (gp[1, halves[0], :].astype(F32) + x2[0].astype(F32)).astype(BF16)
            near.append(send(gp.at[1, halves[0]], x1.at[0, halves[0]], "dp", right))
            far_left[i].wait_recv()
            gp[3, halves[1], :] = (gp[3, halves[1], :].astype(F32) + x2[1].astype(F32)).astype(BF16)
            near.append(send(gp.at[3, halves[1]], x1.at[1, halves[1]], "dp", left))

    def combine(b, part):
        arrive(back_rows[b, part])
        take = pb[b]
        batch = slice(b * GROUP, (b + 1) * GROUP)
        start, total = ((0, pm), (NEXT, pt))[part]
        for i in range(D // TILE):
            got = cb[batch, :, start + i * TILE : start + (i + 1) * TILE].reshape(SLOTS, TILE)
            value = dot(take, got, (0, 0))[: 4 * TOKS].reshape(4, TOKS, TILE)
            total[4 * b : 4 * b + 4, :, i * TILE : (i + 1) * TILE] = value
        if part:
            return
        score = jnp.sum(cb[batch, :, D:NEXT].astype(F32), axis=2, keepdims=True)
        spread = jnp.sum(take.astype(F32).reshape(cube) * score, axis=1)
        tiles = comb[b]
        total = jnp.zeros((TOP, LANES), F32)
        for m in range(GROUP):
            hit = tiles[:TOP] == expert_line[m : m + 1, :]
            total = total + jnp.where(hit, spread[m : m + 1, :], 0.0)
        ggp[4 * b] = total
        for j in range(1, 4):
            ggp[4 * b + j] = pltpu.roll(total, LANES - TOKS * j, 1)

    going = {}

    def flow(name, way, k, buf, total, h=0):
        q = HALF + 1 - k
        if q > reach(-way, h):
            return
        cols = slice(None) if name == "g" else slice(h * (D // 2), (h + 1) * (D // 2))
        value = total[POS[(-way * q) % NZ], :, cols]
        if q < reach(-way, h):
            going[name, way, h, q + 1].wait_recv()
            value = value + buf[q, :, cols].astype(F32)
        buf[q, :, cols] = value.astype(buf.dtype)
        src, dst = buf.at[q], buf.at[q - 1]
        if name != "g":
            src, dst = src.at[:, half_cols[h]], dst.at[:, half_cols[h]]
        going[name, way, h, q] = send(src, dst, "expert", down if way < 0 else up)

    def mixed_step(k):
        for h in range(2):
            flow("m", -1, k, dm, pm, h)
            flow("m", 1, k, um, pm, h)

    def token_step(k):
        flow("g", -1, k, dg, ggp)
        flow("g", 1, k, ug, ggp)
        for h in range(2):
            flow("t", -1, k, dd, pt, h)
            flow("t", 1, k, ud, pt, h)

    settled = []

    def settle(count):
        for copy in started[len(settled) : count]:
            copy.wait_send()
            settled.append(copy)

    back_rows = {}
    scale = gb[:, :1]
    for i in range(NX):
        out = (dot(hs[...], wdf[i], (1, 1)) * scale).astype(BF16)
        ob[:, :, i * TILE : (i + 1) * TILE] = out.reshape(ROWS // 8, 8, TILE)
    back_rows[3, 0] = send_back(3, 0)
    far_grads()
    for i in range(NX):
        back = dot(pair[...], wgf[i], (1, 1)).astype(BF16)
        ob[:, :, NEXT + i * TILE : NEXT + (i + 1) * TILE] = back.reshape(ROWS // 8, 8, TILE)
    back_rows[3, 1] = send_back(3, 1)
    back_rows[2, 0] = send_back(2, 0)
    back_rows[2, 1] = send_back(2, 1)
    combine(3, 0)
    mixed_step(1)
    combine(3, 1)
    token_step(1)
    back_rows[1, 0] = send_back(1, 0)
    back_rows[1, 1] = send_back(1, 1)
    right_grads()
    mixed_step(2)
    left_grads()
    token_step(2)
    combine(2, 0)
    mixed_step(3)
    combine(2, 1)
    token_step(3)
    back_rows[0, 0] = send_back(0, 0)
    back_rows[0, 1] = send_back(0, 1)
    mixed_step(4)
    weight_grads(0)
    token_step(4)
    combine(1, 0)
    pass_grads()
    mixed_step(5)
    combine(1, 1)
    token_step(5)
    settle(n_first // 2)
    mixed_step(6)
    settle(n_first)
    token_step(6)
    combine(0, 0)
    mixed_step(7)
    combine(0, 1)
    token_step(7)
    settle(len(started) - 80)
    mixed_step(8)
    settle(len(started) - 40)
    token_step(8)

    leaving = []

    def leave(src, dst):
        leaving.append(pltpu.make_async_copy(src, dst, local_sem.at[len(leaving)]))
        leaving[-1].start()

    for copy in near:
        copy.wait_recv()
    for (gp, x2, x1), out in zip(grads, (ggu, gd)):
        for at in halves:
            gp[0, at, :] = (
                gp[0, at, :].astype(F32) + x1[0, at, :].astype(F32) + x1[1, at, :].astype(F32)
            ).astype(BF16)
            leave(gp.at[0, at], out.at[0, at])
    for key, copy in going.items():
        if key[-1] == 1:
            copy.wait_recv()
    fm[...] = (pm[home] + dm[0].astype(F32) + um[0].astype(F32)).astype(BF16)
    leave(fm, mixed)
    ft[...] = (pt[home] + dd[0].astype(F32) + ud[0].astype(F32)).astype(BF16)
    leave(ft, gtok)
    gg[...] = ggp[home] + dg[0] + ug[0]
    settle(len(started))
    for copy in leaving:
        copy.wait()


def hand_over(m, t, g, u, d, m_out, t_out, g_out, u_out, d_out, mv, tv, uv, dv, sem, sem_out):
    cut = [pl.ds(i * (SHARD // 4), SHARD // 4) for i in range(4)]
    trips = [(u.at[0, at], uv.at[0, at], u_out.at[0, at]) for at in cut]
    trips += [(d.at[0, at], dv.at[0, at], d_out.at[0, at]) for at in cut]
    trips += [(m, mv, m_out), (t, tv, t_out)]
    loads = [pltpu.make_async_copy(a, v, sem.at[i]) for i, (a, v, o) in enumerate(trips)]
    for copy in loads:
        copy.start()
    g_out[...] = g[:, :TOKS]
    stores = []
    for i, (a, v, o) in enumerate(trips):
        loads[i].wait()
        stores.append(pltpu.make_async_copy(v, o, sem_out.at[i]))
        stores[i].start()
    for copy in stores:
        copy.wait()


def body(tokens, route_ids, gates, cotangent, w_gate_up, w_down):
    vmem = pl.BlockSpec(memory_space=pltpu.VMEM)
    hbm = pl.BlockSpec(memory_space=pl.ANY)
    out = pl.pallas_call(
        kernel,
        out_shape=(
            jax.ShapeDtypeStruct((TOKS, D), BF16),
            jax.ShapeDtypeStruct((TOKS, D), BF16),
            jax.ShapeDtypeStruct((TOP, LANES), F32),
            jax.ShapeDtypeStruct((1, SHARD, 2 * FFW), BF16),
            jax.ShapeDtypeStruct((1, SHARD, FFW), BF16),
        ),
        in_specs=[hbm, hbm, vmem, vmem, hbm, hbm],
        out_specs=[hbm, hbm, vmem, hbm, hbm],
        scratch_shapes=[
            pltpu.VMEM((NZ, TOKS, D), BF16),
            pltpu.VMEM((NZ, TOKS, D), BF16),
            pltpu.VMEM((NZ, 2 * TOP, LANES), F32),
            pltpu.VMEM((BATCHES, 2 * TOP, LANES), F32),
            pltpu.VMEM((BATCHES, SLOTS, LANES), BF16),
            pltpu.VMEM((ROWS // 8, 8, WIDE), BF16),
            pltpu.VMEM((ROWS // 8, 8, WIDE), BF16),
            pltpu.VMEM((NX, SHARD, 2 * FFW), BF16),
            pltpu.VMEM((NX, SHARD, FFW), BF16),
            pltpu.VMEM((ROWS, 2 * FFW), F32),
            pltpu.VMEM((ROWS, FFW), F32),
            pltpu.VMEM((ROWS, LANES), F32),
            pltpu.VMEM((ROWS, FFW), BF16),
            pltpu.VMEM((ROWS, 2 * FFW), BF16),
            pltpu.VMEM((ROWS // 8, 8, WIDE), BF16),
            pltpu.VMEM((ROWS // 8, 8, WIDE), BF16),
            pltpu.VMEM((NZ, TOKS, D), F32),
            pltpu.VMEM((NZ, TOKS, D), F32),
            pltpu.VMEM((NZ, TOP, LANES), F32),
            pltpu.VMEM((HALF + 1, TOKS, D), BF16),
            pltpu.VMEM((HALF + 1, TOKS, D), BF16),
            pltpu.VMEM((HALF + 1, TOKS, D), BF16),
            pltpu.VMEM((HALF + 1, TOKS, D), BF16),
            pltpu.VMEM((HALF + 1, TOP, LANES), F32),
            pltpu.VMEM((HALF, TOP, LANES), F32),
            pltpu.VMEM((NX, SHARD, 2 * FFW), BF16),
            pltpu.VMEM((NX, SHARD, FFW), BF16),
            pltpu.VMEM((2, SHARD // 2, 2 * FFW), BF16),
            pltpu.VMEM((2, SHARD // 2, FFW), BF16),
            pltpu.VMEM((2, SHARD, 2 * FFW), BF16),
            pltpu.VMEM((2, SHARD, FFW), BF16),
            pltpu.VMEM((TOKS, D), BF16),
            pltpu.VMEM((TOKS, D), BF16),
            pltpu.SemaphoreType.DMA((N_SEM,)),
            pltpu.SemaphoreType.DMA((N_SEM,)),
            pltpu.SemaphoreType.DMA((4 + 4 * BATCHES,)),
        ],
        compiler_params=pltpu.CompilerParams(
            collective_id=0, has_side_effects=True, vmem_limit_bytes=60 * 1024 * 1024
        ),
        name="routed_layer",
    )(tokens, cotangent, route_ids.T, gates.T, w_gate_up, w_down)
    specs = [hbm, hbm, vmem, hbm, hbm]
    mixed, grad_tokens, grad_gates, grad_gate_up, grad_down = pl.pallas_call(
        hand_over,
        out_shape=(
            jax.ShapeDtypeStruct((TOKS, D), BF16),
            jax.ShapeDtypeStruct((TOKS, D), BF16),
            jax.ShapeDtypeStruct((TOP, TOKS), F32),
            jax.ShapeDtypeStruct((1, SHARD, 2 * FFW), BF16),
            jax.ShapeDtypeStruct((1, SHARD, FFW), BF16),
        ),
        in_specs=specs,
        out_specs=specs,
        scratch_shapes=[
            pltpu.VMEM((TOKS, D), BF16),
            pltpu.VMEM((TOKS, D), BF16),
            pltpu.VMEM((1, SHARD, 2 * FFW), BF16),
            pltpu.VMEM((1, SHARD, FFW), BF16),
            pltpu.SemaphoreType.DMA((10,)),
            pltpu.SemaphoreType.DMA((10,)),
        ],
        name="hand_over",
    )(*out)
    return mixed, grad_tokens, grad_gates.T, grad_gate_up, grad_down


def solution(mesh):
    rows_spec = P(("expert", "dp"), None)
    weight_spec = P("expert", "dp", None)
    return jax.shard_map(
        body,
        mesh=mesh,
        in_specs=(rows_spec, rows_spec, rows_spec, rows_spec, weight_spec, weight_spec),
        out_specs=(rows_spec, rows_spec, rows_spec, weight_spec, weight_spec),
        check_vma=False,
    )
```

```python
import jax
import jax.numpy as jnp
from jax import lax
from jax.experimental import pallas as pl
from jax.experimental.pallas import tpu as pltpu
from jax.sharding import PartitionSpec as P

NX, NY, NZ, NC = 4, 4, 16, 2
GROUP = NY * NC
HALF = NZ // 2
BATCHES = NZ // 4
PAIR = 2
TOKS = 24
TOP = 8
D = 2048
FFW = 384
LANES = 128
TILE = 512
NEXT = D + LANES
WIDE = D + NEXT
SHARD = D // NX
SLOTS = GROUP * 4 * PAIR
ROWS = BATCHES * SLOTS
N_SEM = 296
F32 = jnp.float32
BF16 = jnp.bfloat16


def positions():
    order = []
    for b in range(BATCHES):
        s = 2 * b + 1
        order += [s, NZ - s, s + 1, NZ - s - 1 if s + 1 < HALF else 0]
    return {d: i for i, d in enumerate(order)}


POS = positions()


def dot(a, b, contract):
    return lax.dot_general(a, b, ((contract[:1], contract[1:]), ((), ())), preferred_element_type=F32)


def columns(i, start=0):
    return pl.ds(pl.multiple_of(start + i * TILE, LANES), TILE)


def three_parts(v):
    high = v.astype(BF16).astype(F32)
    rest = v - high
    middle = rest.astype(BF16).astype(F32)
    return high, middle, rest - middle


def lane_block(v, shape):
    high, middle, low = three_parts(v)
    lane = lax.broadcasted_iota(jnp.int32, shape, len(shape) - 1)
    return jnp.where(
        lane == 0, high, jnp.where(lane == 1, middle, jnp.where(lane == 2, low, 0.0))
    ).astype(BF16)


def kernel(
    tok, cot, ids, gates, wg, wd,
    mixed, gtok, gg, ggu, gd,
    gx, gc, mb, comb, pb, sel, rows, wgf, wdf, pre, ub, gb, hs, pair, ob, cb,
    pm, pt, ggp, dm, um, dd, ud, dg, ug, gp_gu, gp_d, x2_gu, x2_d, x1_gu, x1_d, fm, ft,
    send_sem, recv_sem, local_sem,
):
    e = lax.axis_index("expert")
    x = lax.axis_index("dp")
    plane = NZ * NC
    y = e // plane
    z = (e // NC) % NZ
    c = e % NC
    me = y * NC + c
    up = y * plane + ((z + 1) % NZ) * NC + c
    down = y * plane + ((z + NZ - 1) % NZ) * NC + c
    right = (x + 1) % NX
    left = (x + NX - 1) % NX

    def member(m):
        return (m // NC) * plane + z * NC + m % NC

    barrier = pltpu.get_barrier_semaphore()
    peers = [("expert", up), ("expert", down), ("dp", right), ("dp", left)]
    peers += [("expert", member((me + o) % GROUP)) for o in range(1, GROUP)]
    for axis, target in peers:
        pl.semaphore_signal(
            barrier, inc=1, device_id={axis: target}, device_id_type=pl.DeviceIdType.MESH
        )
    pl.semaphore_wait(barrier, len(peers))

    started = []

    def send(src, dst, axis, target):
        i = len(started)
        copy = pltpu.make_async_remote_copy(
            src_ref=src,
            dst_ref=dst,
            send_sem=send_sem.at[i],
            recv_sem=recv_sem.at[i],
            device_id={axis: target},
            device_id_type=pl.DeviceIdType.MESH,
        )
        copy.start()
        started.append(copy)
        return copy

    halves = [pl.ds(h * (SHARD // 2), SHARD // 2) for h in range(2)]
    half_cols = [pl.ds(h * (D // 2), D // 2) for h in range(2)]
    home = POS[0]
    mb[home] = jnp.zeros((2 * TOP, LANES), F32)
    mb[home, :TOP, :TOKS] = ids[...].astype(F32) + 1.0
    mb[home, TOP:, :TOKS] = gates[...]
    chunks = [("x", 0, tok, gx), ("x", 1, tok, gx), ("m", 0, mb.at[home], mb)]
    chunks += [("c", 0, cot, gc), ("c", 1, cot, gc)]
    ring = {}

    def reach(way, h):
        return HALF if (way > 0) == (h == 0) else HALF - 1

    def ring_send(s):
        for name, h, own, buf in chunks:
            for way, target in ((1, up), (-1, down)):
                if s > reach(way, h):
                    continue
                src, dst = own, buf.at[POS[(way * s) % NZ]]
                if s > 1:
                    ring[name, h, way, s - 1].wait_recv()
                    src = buf.at[POS[(way * (s - 1)) % NZ]]
                if name != "m":
                    src, dst = src.at[:, half_cols[h]], dst.at[:, half_cols[h]]
                ring[name, h, way, s] = send(src, dst, "expert", target)

    def ring_wait(name):
        for h in range(1 if name == "m" else 2):
            ring[name, h, 1, reach(1, h)].wait_recv()
            ring[name, h, -1, reach(-1, h)].wait_recv()

    ring_send(1)

    weights = ((wg, wgf), (wd, wdf))
    to_right, to_left = {}, {}
    for h in range(2):
        for i, (w, full) in enumerate(weights):
            to_right[i, h] = send(w.at[0, halves[h]], full.at[x, halves[h]], "dp", right)
            g = 1 - h
            to_left[i, g] = send(w.at[0, halves[g]], full.at[x, halves[g]], "dp", left)
    keep = [
        pltpu.make_async_copy(w.at[0], full.at[x], local_sem.at[i])
        for i, (w, full) in enumerate(weights)
    ]
    keep.append(pltpu.make_async_copy(tok, gx.at[home], local_sem.at[2]))
    keep.append(pltpu.make_async_copy(cot, gc.at[home], local_sem.at[3]))
    for copy in keep:
        copy.start()
    on_right, on_left = {}, {}

    def pass_weights():
        for i, (w, full) in enumerate(weights):
            to_right[i, 0].wait_recv()
            piece = full.at[left, halves[0]]
            on_right[i] = send(piece, piece, "dp", right)
            to_left[i, 1].wait_recv()
            piece = full.at[right, halves[1]]
            on_left[i] = send(piece, piece, "dp", left)


    lane = lax.broadcasted_iota(jnp.int32, (LANES, LANES), 1)
    line = lax.broadcasted_iota(jnp.int32, (LANES, LANES), 0)

    def source_of(index):
        total = jnp.zeros(index.shape, jnp.int32)
        for j in range(1, 5):
            total = total + jnp.where(index >= j * TOKS, 1, 0)
        return total

    earlier = jnp.where((line < lane) & (source_of(line) == source_of(lane)), 1.0, 0.0).astype(F32)
    member_line = lax.broadcasted_iota(jnp.int32, (GROUP, LANES), 0)
    expert_line = ((member_line >> 1) * plane + z * NC + (member_line & 1) + 1).astype(F32)
    cube = (GROUP, 4 * PAIR, LANES)
    cube_row = lax.broadcasted_iota(jnp.int32, cube, 1)
    cube_source = source_of(lax.broadcasted_iota(jnp.int32, cube, 2))

    def choose(b):
        tiles = mb[4 * b]
        for j in range(1, 4):
            tiles = tiles + pltpu.roll(mb[4 * b + j], TOKS * j, 1)
        comb[b] = tiles
        hits = jnp.zeros((GROUP, LANES), F32)
        gate = jnp.zeros((GROUP, LANES), F32)
        for k in range(TOP):
            hit = tiles[k : k + 1, :] == expert_line
            hits = hits + jnp.where(hit, 1.0, 0.0)
            gate = gate + jnp.where(hit, tiles[TOP + k : TOP + k + 1, :], 0.0)
        count = dot(hits, earlier, (1, 0))
        wanted = (cube_row >> 1) == cube_source
        turn = (cube_row & 1).astype(F32)
        chosen = jnp.where(
            wanted & (jnp.broadcast_to(count[:, None, :], cube) == turn),
            jnp.broadcast_to(hits[:, None, :], cube),
            0.0,
        )
        pb[b] = chosen.reshape(SLOTS, LANES).astype(BF16)
        weight = jnp.sum(chosen * gate[:, None, :], axis=2, keepdims=True)
        sel[b * GROUP : (b + 1) * GROUP, :, D:NEXT] = lane_block(weight, cube)

    def pick(b, buf, offset):
        take = pb[b][:, : 4 * TOKS]
        batch = slice(b * GROUP, (b + 1) * GROUP)
        weight = jnp.sum(sel[batch, :, D:NEXT].astype(F32), axis=2, keepdims=True)
        for i in range(D // TILE):
            block = buf[4 * b : 4 * b + 4, :, i * TILE : (i + 1) * TILE].reshape(4 * TOKS, TILE)
            got = dot(take, block, (1, 0)).reshape(GROUP, 4 * PAIR, TILE)
            if offset:
                got = got * weight
            sel[batch, :, offset + i * TILE : offset + (i + 1) * TILE] = got.astype(BF16)

    parts = (pl.ds(0, NEXT), pl.ds(NEXT, D))

    def exchange(b, src, dst, part, sem):
        copies = []
        for o in range(1, GROUP):
            m = (me + o) % GROUP
            copies.append(
                send(
                    src.at[b * GROUP + m, :, parts[part]],
                    dst.at[b * GROUP + me, :, parts[part]],
                    "expert",
                    member(m),
                )
            )
        own = pltpu.make_async_copy(
            src.at[b * GROUP + me, :, parts[part]],
            dst.at[b * GROUP + me, :, parts[part]],
            local_sem.at[sem],
        )
        own.start()
        return copies, own

    def arrive(exchanged):
        for copy in exchanged[0]:
            copy.wait_recv()
        exchanged[1].wait()

    out_rows = {}
    for s in range(2, HALF + 1):
        ring_send(s)
        if s >= 3:
            b = (s - 3) // 2
            if s % 2:
                choose(b)
                pick(b, gx, 0)
                out_rows[b, 0] = exchange(b, sel, rows, 0, 4 + 2 * b)
            else:
                pick(b, gc, NEXT)
                out_rows[b, 1] = exchange(b, sel, rows, 1, 5 + 2 * b)
        if s == 5:
            pass_weights()
    last = BATCHES - 1
    for copy in keep:
        copy.wait()
    ring_wait("m")
    choose(last)
    ring_wait("x")
    pick(last, gx, 0)
    out_rows[last, 0] = exchange(last, sel, rows, 0, 4 + 2 * last)
    ring_wait("c")
    pick(last, gc, NEXT)
    out_rows[last, 1] = exchange(last, sel, rows, 1, 5 + 2 * last)
    n_first = len(started)

    def take_rows(i, start=0):
        return rows[:, :, columns(i, start)].reshape(ROWS, TILE)

    def gate_up_product(slot, first):
        value = dot(take_rows(slot), wgf[slot], (1, 0))
        pre[...] = value if first else pre[...] + value

    def down_product(slot, first):
        value = dot(take_rows(slot, NEXT), wdf[slot], (1, 0))
        ub[...] = value if first else ub[...] + value

    for b in range(BATCHES):
        arrive(out_rows[b, 0])
    gate_up_product(x, True)
    for i in range(2):
        to_right[i, 1].wait_recv()
        to_left[i, 0].wait_recv()
    gate_up_product(left, False)
    gate_up_product(right, False)
    for i in range(2):
        on_right[i].wait_recv()
        on_left[i].wait_recv()
    gate_up_product((x + 2) % NX, False)
    for b in range(BATCHES):
        arrive(out_rows[b, 1])
    down_product(0, True)
    for i in range(1, NX):
        down_product(i, False)

    step_rows = 32

    @pl.loop(0, ROWS // step_rows)
    def _(i):
        at = pl.ds(pl.multiple_of(i * step_rows, step_rows), step_rows)
        blocks = pl.ds(i * (step_rows // 8), step_rows // 8)
        gate_pre = pre[at, :FFW]
        up_pre = pre[at, FFW:]
        back = ub[at, :]
        weight = jnp.sum(
            rows[blocks, :, D:NEXT].astype(F32).reshape(step_rows, LANES), axis=1, keepdims=True
        )
        sigmoid_gate = jax.nn.sigmoid(gate_pre)
        activation = gate_pre * sigmoid_gate
        hidden = activation * up_pre
        gb[at, :] = jnp.broadcast_to(weight, (step_rows, LANES))
        hs[at, :] = hidden.astype(BF16)
        pair[at, :FFW] = (
            back * up_pre * (sigmoid_gate * (1.0 + gate_pre * (1.0 - sigmoid_gate)))
        ).astype(BF16)
        pair[at, FFW:] = (back * activation).astype(BF16)
        score = jnp.sum(hidden * back, axis=1, keepdims=True)
        score = score / jnp.where(weight > 0.0, weight, 1.0)
        ob[blocks, :, D:NEXT] = lane_block(score, (step_rows, LANES)).reshape(
            step_rows // 8, 8, LANES
        )

    def send_back(b, part):
        return exchange(b, ob, cb, part, 4 + 2 * BATCHES + 2 * b + part)

    def weight_grads(o):
        slot = (x + o) % NX
        gp_gu[o] = dot(take_rows(slot), pair[...], (0, 0)).astype(BF16)
        gp_d[o] = dot(take_rows(slot, NEXT), hs[...], (0, 0)).astype(BF16)

    grads = ((gp_gu, x2_gu, x1_gu), (gp_d, x2_d, x1_d))
    far_right, far_left, near = [], [], []

    def far_grads():
        slot = (x + 2) % NX
        size = SHARD // 2
        for start, right_side, (gp, x2, x1) in zip((0, NEXT), (pair, hs), grads):
            for h, target, sent in ((0, right, far_right), (1, left, far_left)):
                at = pl.ds(pl.multiple_of(start + slot * SHARD + h * size, LANES), size)
                piece = rows[:, :, at].reshape(ROWS, size)
                gp[2, halves[h], :] = dot(piece, right_side[...], (0, 0)).astype(BF16)
                sent.append(send(gp.at[2, halves[h]], x2.at[h], "dp", target))

    def right_grads():
        weight_grads(1)
        for gp, x2, x1 in grads:
            near.append(send(gp.at[1, halves[1]], x1.at[0, halves[1]], "dp", right))

    def left_grads():
        weight_grads(3)
        for gp, x2, x1 in grads:
            near.append(send(gp.at[3, halves[0]], x1.at[1, halves[0]], "dp", left))

    def pass_grads():
        for i, (gp, x2, x1) in enumerate(grads):
            far_right[i].wait_recv()
            gp[1, halves[0], :] = (gp[1, halves[0], :].astype(F32) + x2[0].astype(F32)).astype(BF16)
            near.append(send(gp.at[1, halves[0]], x1.at[0, halves[0]], "dp", right))
            far_left[i].wait_recv()
            gp[3, halves[1], :] = (gp[3, halves[1], :].astype(F32) + x2[1].astype(F32)).astype(BF16)
            near.append(send(gp.at[3, halves[1]], x1.at[1, halves[1]], "dp", left))

    def combine(b, part):
        arrive(back_rows[b, part])
        take = pb[b]
        batch = slice(b * GROUP, (b + 1) * GROUP)
        start, total = ((0, pm), (NEXT, pt))[part]
        for i in range(D // TILE):
            got = cb[batch, :, start + i * TILE : start + (i + 1) * TILE].reshape(SLOTS, TILE)
            value = dot(take, got, (0, 0))[: 4 * TOKS].reshape(4, TOKS, TILE)
            total[4 * b : 4 * b + 4, :, i * TILE : (i + 1) * TILE] = value
        if part:
            return
        score = jnp.sum(cb[batch, :, D:NEXT].astype(F32), axis=2, keepdims=True)
        spread = jnp.sum(take.astype(F32).reshape(cube) * score, axis=1)
        tiles = comb[b]
        total = jnp.zeros((TOP, LANES), F32)
        for m in range(GROUP):
            hit = tiles[:TOP] == expert_line[m : m + 1, :]
            total = total + jnp.where(hit, spread[m : m + 1, :], 0.0)
        ggp[4 * b] = total
        for j in range(1, 4):
            ggp[4 * b + j] = pltpu.roll(total, LANES - TOKS * j, 1)

    going = {}

    def flow(name, way, k, buf, total, h=0):
        q = HALF + 1 - k
        if q > reach(-way, h):
            return
        cols = slice(None) if name == "g" else slice(h * (D // 2), (h + 1) * (D // 2))
        value = total[POS[(-way * q) % NZ], :, cols]
        if q < reach(-way, h):
            going[name, way, h, q + 1].wait_recv()
            value = value + buf[q, :, cols].astype(F32)
        buf[q, :, cols] = value.astype(buf.dtype)
        src, dst = buf.at[q], buf.at[q - 1]
        if name != "g":
            src, dst = src.at[:, half_cols[h]], dst.at[:, half_cols[h]]
        going[name, way, h, q] = send(src, dst, "expert", down if way < 0 else up)

    def mixed_step(k):
        for h in range(2):
            flow("m", -1, k, dm, pm, h)
            flow("m", 1, k, um, pm, h)

    def token_step(k):
        for h in range(2):
            flow("t", -1, k, dd, pt, h)
            flow("t", 1, k, ud, pt, h)
        flow("g", -1, k, dg, ggp)
        flow("g", 1, k, ug, ggp)

    settled = []

    def settle(count):
        for copy in started[len(settled) : count]:
            copy.wait_send()
            settled.append(copy)

    back_rows = {}
    scale = gb[:, :1]
    for i in range(NX):
        out = (dot(hs[...], wdf[i], (1, 1)) * scale).astype(BF16)
        ob[:, :, i * TILE : (i + 1) * TILE] = out.reshape(ROWS // 8, 8, TILE)
    back_rows[3, 0] = send_back(3, 0)
    far_grads()
    for i in range(NX):
        back = dot(pair[...], wgf[i], (1, 1)).astype(BF16)
        ob[:, :, NEXT + i * TILE : NEXT + (i + 1) * TILE] = back.reshape(ROWS // 8, 8, TILE)
    back_rows[3, 1] = send_back(3, 1)
    combine(3, 0)
    mixed_step(1)
    back_rows[2, 0] = send_back(2, 0)
    back_rows[2, 1] = send_back(2, 1)
    combine(3, 1)
    token_step(1)
    back_rows[1, 0] = send_back(1, 0)
    back_rows[1, 1] = send_back(1, 1)
    right_grads()
    mixed_step(2)
    left_grads()
    token_step(2)
    combine(2, 0)
    mixed_step(3)
    combine(2, 1)
    token_step(3)
    back_rows[0, 0] = send_back(0, 0)
    back_rows[0, 1] = send_back(0, 1)
    mixed_step(4)
    weight_grads(0)
    token_step(4)
    combine(1, 0)
    pass_grads()
    mixed_step(5)
    combine(1, 1)
    token_step(5)
    settle(n_first // 2)
    mixed_step(6)
    settle(n_first)
    token_step(6)
    combine(0, 0)
    mixed_step(7)
    combine(0, 1)
    token_step(7)
    settle(len(started) - 80)
    mixed_step(8)
    settle(len(started) - 40)
    token_step(8)

    leaving = []

    def leave(src, dst):
        leaving.append(pltpu.make_async_copy(src, dst, local_sem.at[len(leaving)]))
        leaving[-1].start()

    for copy in near:
        copy.wait_recv()
    for (gp, x2, x1), out in zip(grads, (ggu, gd)):
        for at in halves:
            gp[0, at, :] = (
                gp[0, at, :].astype(F32) + x1[0, at, :].astype(F32) + x1[1, at, :].astype(F32)
            ).astype(BF16)
            leave(gp.at[0, at], out.at[0, at])
    for key, copy in going.items():
        if key[-1] == 1:
            copy.wait_recv()
    fm[...] = (pm[home] + dm[0].astype(F32) + um[0].astype(F32)).astype(BF16)
    leave(fm, mixed)
    ft[...] = (pt[home] + dd[0].astype(F32) + ud[0].astype(F32)).astype(BF16)
    leave(ft, gtok)
    gg[...] = ggp[home] + dg[0] + ug[0]
    settle(len(started))
    for copy in leaving:
        copy.wait()


def hand_over(m, t, g, u, d, m_out, t_out, g_out, u_out, d_out, mv, tv, uv, dv, sem, sem_out):
    cut = [pl.ds(i * (SHARD // 4), SHARD // 4) for i in range(4)]
    trips = [(u.at[0, at], uv.at[0, at], u_out.at[0, at]) for at in cut]
    trips += [(d.at[0, at], dv.at[0, at], d_out.at[0, at]) for at in cut]
    trips += [(m, mv, m_out), (t, tv, t_out)]
    loads = [pltpu.make_async_copy(a, v, sem.at[i]) for i, (a, v, o) in enumerate(trips)]
    for copy in loads:
        copy.start()
    g_out[...] = g[:, :TOKS]
    stores = []
    for i, (a, v, o) in enumerate(trips):
        loads[i].wait()
        stores.append(pltpu.make_async_copy(v, o, sem_out.at[i]))
        stores[i].start()
    for copy in stores:
        copy.wait()


def body(tokens, route_ids, gates, cotangent, w_gate_up, w_down):
    vmem = pl.BlockSpec(memory_space=pltpu.VMEM)
    hbm = pl.BlockSpec(memory_space=pl.ANY)
    out = pl.pallas_call(
        kernel,
        out_shape=(
            jax.ShapeDtypeStruct((TOKS, D), BF16),
            jax.ShapeDtypeStruct((TOKS, D), BF16),
            jax.ShapeDtypeStruct((TOP, LANES), F32),
            jax.ShapeDtypeStruct((1, SHARD, 2 * FFW), BF16),
            jax.ShapeDtypeStruct((1, SHARD, FFW), BF16),
        ),
        in_specs=[hbm, hbm, vmem, vmem, hbm, hbm],
        out_specs=[hbm, hbm, vmem, hbm, hbm],
        scratch_shapes=[
            pltpu.VMEM((NZ, TOKS, D), BF16),
            pltpu.VMEM((NZ, TOKS, D), BF16),
            pltpu.VMEM((NZ, 2 * TOP, LANES), F32),
            pltpu.VMEM((BATCHES, 2 * TOP, LANES), F32),
            pltpu.VMEM((BATCHES, SLOTS, LANES), BF16),
            pltpu.VMEM((ROWS // 8, 8, WIDE), BF16),
            pltpu.VMEM((ROWS // 8, 8, WIDE), BF16),
            pltpu.VMEM((NX, SHARD, 2 * FFW), BF16),
            pltpu.VMEM((NX, SHARD, FFW), BF16),
            pltpu.VMEM((ROWS, 2 * FFW), F32),
            pltpu.VMEM((ROWS, FFW), F32),
            pltpu.VMEM((ROWS, LANES), F32),
            pltpu.VMEM((ROWS, FFW), BF16),
            pltpu.VMEM((ROWS, 2 * FFW), BF16),
            pltpu.VMEM((ROWS // 8, 8, WIDE), BF16),
            pltpu.VMEM((ROWS // 8, 8, WIDE), BF16),
            pltpu.VMEM((NZ, TOKS, D), F32),
            pltpu.VMEM((NZ, TOKS, D), F32),
            pltpu.VMEM((NZ, TOP, LANES), F32),
            pltpu.VMEM((HALF + 1, TOKS, D), BF16),
            pltpu.VMEM((HALF + 1, TOKS, D), BF16),
            pltpu.VMEM((HALF + 1, TOKS, D), BF16),
            pltpu.VMEM((HALF + 1, TOKS, D), BF16),
            pltpu.VMEM((HALF + 1, TOP, LANES), F32),
            pltpu.VMEM((HALF, TOP, LANES), F32),
            pltpu.VMEM((NX, SHARD, 2 * FFW), BF16),
            pltpu.VMEM((NX, SHARD, FFW), BF16),
            pltpu.VMEM((2, SHARD // 2, 2 * FFW), BF16),
            pltpu.VMEM((2, SHARD // 2, FFW), BF16),
            pltpu.VMEM((2, SHARD, 2 * FFW), BF16),
            pltpu.VMEM((2, SHARD, FFW), BF16),
            pltpu.VMEM((TOKS, D), BF16),
            pltpu.VMEM((TOKS, D), BF16),
            pltpu.SemaphoreType.DMA((N_SEM,)),
            pltpu.SemaphoreType.DMA((N_SEM,)),
            pltpu.SemaphoreType.DMA((4 + 4 * BATCHES,)),
        ],
        compiler_params=pltpu.CompilerParams(
            collective_id=0, has_side_effects=True, vmem_limit_bytes=60 * 1024 * 1024
        ),
        name="routed_layer",
    )(tokens, cotangent, route_ids.T, gates.T, w_gate_up, w_down)
    specs = [hbm, hbm, vmem, hbm, hbm]
    mixed, grad_tokens, grad_gates, grad_gate_up, grad_down = pl.pallas_call(
        hand_over,
        out_shape=(
            jax.ShapeDtypeStruct((TOKS, D), BF16),
            jax.ShapeDtypeStruct((TOKS, D), BF16),
            jax.ShapeDtypeStruct((TOP, TOKS), F32),
            jax.ShapeDtypeStruct((1, SHARD, 2 * FFW), BF16),
            jax.ShapeDtypeStruct((1, SHARD, FFW), BF16),
        ),
        in_specs=specs,
        out_specs=specs,
        scratch_shapes=[
            pltpu.VMEM((TOKS, D), BF16),
            pltpu.VMEM((TOKS, D), BF16),
            pltpu.VMEM((1, SHARD, 2 * FFW), BF16),
            pltpu.VMEM((1, SHARD, FFW), BF16),
            pltpu.SemaphoreType.DMA((10,)),
            pltpu.SemaphoreType.DMA((10,)),
        ],
        name="hand_over",
    )(*out)
    return mixed, grad_tokens, grad_gates.T, grad_gate_up, grad_down


def solution(mesh):
    rows_spec = P(("expert", "dp"), None)
    weight_spec = P("expert", "dp", None)
    return jax.shard_map(
        body,
        mesh=mesh,
        in_specs=(rows_spec, rows_spec, rows_spec, rows_spec, weight_spec, weight_spec),
        out_specs=(rows_spec, rows_spec, rows_spec, weight_spec, weight_spec),
        check_vma=False,
    )
```
